32 devices in a mesh: chan: 4 (over x, core), slab: 8 (over z, y).
Axes of the slice: x: 2, y: 2, z: 4, core: 2. Of those that a mesh axis runs over, the one named last changes fastest.
Arguments:
- image: float32 [4, 1024, 1024], P('chan', 'slab'), may hold values from 0 to 2
- margin: int32 [8], P('slab'), may hold values from 1 to 3
- cells: int32 [4, 32768], P('chan', 'slab'), may hold values from 1 to 131071
- weights: float32 [4, 32768], P('chan', 'slab'), may hold values from 0.25 to 4
- observed: float32 [2, 4, 32768], P(None, 'chan', 'slab'), may hold values from -6 to 6
- dual_start: float32 [2, 4, 32768], P(None, 'chan', 'slab'), may hold values from -4 to 4
Outputs:
- restored: float32 [4, 1024, 1024], P('chan', 'slab')
- vis_dual: float32 [2, 4, 32768], P(None, 'chan', 'slab')
The draws below stay inside these ranges and needn't reach their ends.
Inputs may be any that keep to these rules, and one draw needn't show every extreme that they name: `cells`: visibility k of a channel belongs to facet s = k div 4096; its value q names frequency column s * 128 + q div 1024 and frequency row q mod 1024.
All inputs are finite; a program needn't handle non-finite values.
Results may differ from the reference program's by a relative error of at most 0.0047.
Values may be sent and summed in bfloat16 or wider, within the bound.
A program may use at most 64 MiB of HBM per device.

```python
import math
import jax
import jax.numpy as jnp
from jax import lax

N = 1024
VIS_DEV = 4096
ITERS = 1
HALO = 3
CHANNELS = 4
FACETS = 8
ROWS_DEV = 128
VISIBILITIES = 32768


def place_ends(result, stream_key, smallest, top_value):
    longest = result.shape.index(max(result.shape))
    spots = []
    for shift in (0, 1):
        where = [jax.random.randint(jax.random.fold_in(stream_key, axis), (), 0, length) for axis, length in enumerate(result.shape)]
        where[longest] = (where[longest] + shift) % result.shape[longest]
        spots.append(tuple(where))
    return result.at[spots[0]].set(smallest).at[spots[1]].set(top_value)


def block_scale(key, dims, shards, smallest, high):
    loudness = 1.0
    for dim, blocks in shards:
        steps = jax.random.uniform(jax.random.fold_in(jax.random.fold_in(key, 6), dim), (blocks,), jnp.float32, smallest / len(shards), high / len(shards))
        loudness = loudness * jnp.repeat(jnp.exp(steps), dims[dim] // blocks).reshape((-1,) + (1,) * (len(dims) - 1 - dim))
    return loudness


def scatter_about(stream_key, dims, scale, reach, split=(), kind=jnp.bfloat16):
    level = block_scale(stream_key, dims, split, -0.22, 0.18) if split else 1.0
    entries = jax.random.normal(stream_key, dims, jnp.float32) * scale * level
    return jnp.minimum(jnp.maximum(entries, -reach), reach).astype(kind)


def setup_inputs(seed: int = 0) -> dict:
    splits = jax.random.split(jax.random.key(seed), 7)
    return {
        "image": jnp.clip(2.0 * jax.random.uniform(splits[0], (CHANNELS, N, N), jnp.float32) ** block_scale(splits[0], (CHANNELS, N, N), ((0, 4), (1, 8)), -0.2, 0.2), 0.0, 2.0),
        "margin": place_ends(jax.random.randint(splits[1], (FACETS,), 1, HALO + 1), jax.random.fold_in(splits[1], 1), 1, HALO).astype(jnp.int32),
        "cells": place_ends(jax.random.randint(splits[2], (CHANNELS, VISIBILITIES), 1, ROWS_DEV * N), jax.random.fold_in(splits[2], 1), 1, (ROWS_DEV * N) - 1).astype(jnp.int32),
        "weights": jnp.clip(jnp.exp(math.log(4.0) - 2.7725887 * jax.random.uniform(splits[3], (CHANNELS, VISIBILITIES), jnp.float32) ** block_scale(splits[3], (CHANNELS, VISIBILITIES), ((0, 4), (1, 8)), -0.2, 0.2)), 0.25, 4.0),
        "observed": scatter_about(splits[4], (2, CHANNELS, VISIBILITIES), 1.0, 6.0, ((1, 4), (2, 8)), jnp.float32),
        "dual_start": scatter_about(splits[5], (2, CHANNELS, VISIBILITIES), 0.5, 4.0, ((1, 4), (2, 8)), jnp.float32),
    }


low_taps = (-0.010597401784997278, 0.032883011666982945, 0.030841381835986965, -0.18703481171888114, -0.02798376941698385, 0.6308807679295904, 0.7148465705525415, 0.23037781330885523)
high_taps = (-0.23037781330885523, 0.7148465705525415, -0.6308807679295904, -0.02798376941698385, 0.18703481171888114, 0.030841381835986965, -0.032883011666982945, -0.010597401784997278)
tau_step = 0.5
bound_level = 3.0

def tap_value(offset, taps):
    total = jnp.zeros(offset.shape, jnp.float32)
    for position in range(8):
        total = total + jnp.where(offset == position, taps[position], 0.0).astype(jnp.float32)
    return total

def fourier_tables(length):
    index = jnp.arange(length, dtype=jnp.int32)
    product = index[:, None] * index[None, :] % length
    angle = product.astype(jnp.float32) * (2.0 * math.pi / length)
    scale = 1.0 / math.sqrt(length)
    return ((jnp.cos(angle) * scale).astype(jnp.bfloat16), (jnp.sin(angle) * scale).astype(jnp.bfloat16))

def column_matrix(length):
    half = length // 2
    line = jnp.arange(length, dtype=jnp.int32)[:, None]
    column = jnp.arange(length, dtype=jnp.int32)[None, :]
    offset = line - 2 * (column % half) + HALO
    return jnp.where(column < half, tap_value(offset, low_taps), tap_value(offset, high_taps))

def row_matrix(count):
    half = count // 2
    line = jnp.arange(count + 2 * HALO, dtype=jnp.int32)[:, None]
    column = jnp.arange(count, dtype=jnp.int32)[None, :]
    offset = line - 2 * (column % half)
    return jnp.where(column < half, tap_value(offset, low_taps), tap_value(offset, high_taps))

def facet_mask(count, width):
    line = jnp.arange(count + 2 * HALO, dtype=jnp.int32)
    distance = jnp.maximum(jnp.maximum(HALO - line, line - count - HALO + 1), 0)
    return (distance[None, :] <= width[:, None]).astype(jnp.float32)

def forward_grid(plane, cos_table, sin_table):
    flat_b = plane.astype(jnp.bfloat16)
    spec_real = jnp.dot(flat_b, cos_table, preferred_element_type=jnp.float32).astype(jnp.bfloat16)
    spec_imag = (-jnp.dot(flat_b, sin_table, preferred_element_type=jnp.float32)).astype(jnp.bfloat16)
    grid_real = jnp.dot(spec_real.T, cos_table, preferred_element_type=jnp.float32) + jnp.dot(spec_imag.T, sin_table, preferred_element_type=jnp.float32)
    grid_imag = jnp.dot(spec_imag.T, cos_table, preferred_element_type=jnp.float32) - jnp.dot(spec_real.T, sin_table, preferred_element_type=jnp.float32)
    return (grid_real, grid_imag)

def adjoint_grid(hold_real, hold_imag, cos_table, sin_table):
    back_real = (jnp.dot(hold_real, cos_table, preferred_element_type=jnp.float32) - jnp.dot(hold_imag, sin_table, preferred_element_type=jnp.float32)).astype(jnp.bfloat16)
    back_imag = (jnp.dot(hold_real, sin_table, preferred_element_type=jnp.float32) + jnp.dot(hold_imag, cos_table, preferred_element_type=jnp.float32)).astype(jnp.bfloat16)
    return jnp.dot(back_real.T, cos_table, preferred_element_type=jnp.float32) - jnp.dot(back_imag.T, sin_table, preferred_element_type=jnp.float32)

def accumulate(positions, values):
    return jnp.zeros((N * N,), jnp.float32).at[positions].add(values)

def reference(image, margin, cells, weights, observed, dual_start):
    highest = lax.Precision.HIGHEST
    cos_table, sin_table = fourier_tables(N)
    column_map = column_matrix(N)
    row_map = row_matrix(ROWS_DEV)
    mask = facet_mask(ROWS_DEV, margin)
    index = jnp.arange(FACETS, dtype=jnp.int32)[:, None] * ROWS_DEV + jnp.arange(ROWS_DEV + 2 * HALO, dtype=jnp.int32)[None, :]
    offsets = jnp.arange(VISIBILITIES, dtype=jnp.int32) // VIS_DEV * (ROWS_DEV * N)
    place = (cells + offsets[None, :]).astype(jnp.int32)
    estimate = image
    lifted = image
    vis_dual = dual_start
    wave_dual = jnp.zeros((CHANNELS, FACETS, ROWS_DEV, N), jnp.float32)
    for iteration in range(ITERS):
        grid_real, grid_imag = lax.map(lambda plane: forward_grid(plane, cos_table, sin_table), lifted)
        model_real = weights * jnp.take_along_axis(grid_real.reshape(CHANNELS, N * N), place, axis=1)
        model_imag = weights * jnp.take_along_axis(grid_imag.reshape(CHANNELS, N * N), place, axis=1)
        model = jnp.stack([model_real, model_imag])
        vis_dual = (vis_dual + (model - observed)) / 2.0
        hold_real = jax.vmap(accumulate)(place, weights * vis_dual[0]).reshape(CHANNELS, N, N).astype(jnp.bfloat16)
        hold_imag = jax.vmap(accumulate)(place, weights * vis_dual[1]).reshape(CHANNELS, N, N).astype(jnp.bfloat16)
        data_term = lax.map(lambda pair: adjoint_grid(pair[0], pair[1], cos_table, sin_table), (hold_real, hold_imag))
        padded = jnp.pad(lifted, ((0, 0), (HALO, HALO), (0, 0)))
        extended = padded[:, index, :] * mask[None, :, :, None]
        filtered = jnp.einsum('cfen,nm->cfem', extended, column_map, precision=highest)
        coef = jnp.einsum('er,cfem->cfrm', row_map, filtered, precision=highest)
        mixed = wave_dual + coef
        total = lax.optimization_barrier(jnp.sum(mixed * mixed, axis=0))
        factor = bound_level / jnp.maximum(jnp.sqrt(total), bound_level)
        wave_dual = mixed * factor[None]
        back = jnp.einsum('cfrm,nm->cfrn', wave_dual, column_map, precision=highest)
        spread = jnp.einsum('er,cfrn->cfen', row_map, back, precision=highest) * mask[None, :, :, None]
        target = jnp.zeros((CHANNELS, N + 2 * HALO, N), jnp.float32).at[:, index, :].add(spread)
        wave_term = target[:, HALO:N + HALO, :]
        fresh = jnp.maximum(estimate - tau_step * (data_term + wave_term), 0.0)
        lifted = 2.0 * fresh - estimate
        estimate = fresh
    return (estimate, vis_dual)
```

```python
import functools
import math

import jax
import jax.numpy as jnp
import numpy as np
from jax import lax
from jax.experimental import pallas as pl
from jax.experimental.pallas import tpu as pltpu
from jax.sharding import PartitionSpec as P

N = 1024
HALO = 3


low_taps = (
    -0.010597401784997278,
    0.032883011666982945,
    0.030841381835986965,
    -0.18703481171888114,
    -0.02798376941698385,
    0.6308807679295904,
    0.7148465705525415,
    0.23037781330885523,
)
high_taps = (
    -0.23037781330885523,
    0.7148465705525415,
    -0.6308807679295904,
    -0.02798376941698385,
    0.18703481171888114,
    0.030841381835986965,
    -0.032883011666982945,
    -0.010597401784997278,
)
tau_step = 0.5
bound_level = 3.0
leading = (((0,), (0,)), ((), ()))


def with_halo(block, sides, width):
    for axis, dim in sides:
        count = lax.axis_size(axis)
        forward = [(i, i + 1) for i in range(count - 1)]
        backward = [(target, source) for source, target in forward]
        low = lax.ppermute(
            lax.slice_in_dim(block, block.shape[dim] - width, None, axis=dim), axis, forward
        )
        high = lax.ppermute(lax.slice_in_dim(block, 0, width, axis=dim), axis, backward)
        block = jnp.concatenate([low, block, high], axis=dim)
    return block


def tap_value(offset, taps):
    total = jnp.zeros(offset.shape, jnp.float32)
    for position in range(8):
        total = total + jnp.where(offset == position, taps[position], 0.0).astype(jnp.float32)
    return total


def fourier_tables(length):
    index = jnp.arange(length, dtype=jnp.int32)
    product = index[:, None] * index[None, :] % length
    angle = product.astype(jnp.float32) * (2.0 * math.pi / length)
    scale = 1.0 / math.sqrt(length)
    return (
        (jnp.cos(angle) * scale).astype(jnp.bfloat16),
        (jnp.sin(angle) * scale).astype(jnp.bfloat16),
    )


def row_matrix(count):
    half = count // 2
    line = jnp.arange(count + 2 * HALO, dtype=jnp.int32)[:, None]
    column = jnp.arange(count, dtype=jnp.int32)[None, :]
    offset = line - 2 * (column % half)
    return jnp.where(column < half, tap_value(offset, low_taps), tap_value(offset, high_taps))


def facet_mask(count, width):
    line = jnp.arange(count + 2 * HALO, dtype=jnp.int32)
    distance = jnp.maximum(jnp.maximum(HALO - line, line - count - HALO + 1), 0)
    return (distance[None, :] <= width[:, None]).astype(jnp.float32)


def column_forward(values):
    width = values.shape[1]
    half = width // 2
    padded = jnp.pad(values, ((0, 0), (HALO, 8)))
    even_cells = padded[:, 0::2]
    odd_cells = padded[:, 1::2]
    low_part = jnp.zeros((values.shape[0], half), jnp.float32)
    high_part = jnp.zeros((values.shape[0], half), jnp.float32)
    for position in range(8):
        source = even_cells if position % 2 == 0 else odd_cells
        piece = source[:, position // 2 : position // 2 + half]
        low_part = low_part + low_taps[position] * piece
        high_part = high_part + high_taps[position] * piece
    return jnp.concatenate([low_part, high_part], axis=1)


def column_adjoint(coefs):
    width = coefs.shape[1]
    half = width // 2
    low_part = coefs[:, :half]
    high_part = coefs[:, half:]
    even_sums = jnp.zeros((coefs.shape[0], half + 4), jnp.float32)
    odd_sums = jnp.zeros((coefs.shape[0], half + 4), jnp.float32)
    for position in range(8):
        term = low_taps[position] * low_part + high_taps[position] * high_part
        placed = jnp.pad(term, ((0, 0), (position // 2, 4 - position // 2)))
        if position % 2 == 0:
            even_sums = even_sums + placed
        else:
            odd_sums = odd_sums + placed
    joined = jnp.stack([even_sums, odd_sums], axis=2).reshape(coefs.shape[0], width + 8)
    return joined[:, HALO : HALO + width]


def data_part(lifted, dual, seen, places, gains, cos_table, sin_table):
    flat_b = lifted.astype(jnp.bfloat16)
    spectra = jnp.stack(
        [
            jnp.dot(flat_b, cos_table, preferred_element_type=jnp.float32),
            -jnp.dot(flat_b, sin_table, preferred_element_type=jnp.float32),
        ]
    ).astype(jnp.bfloat16)
    columns = lax.all_to_all(spectra, "slab", split_axis=2, concat_axis=1, tiled=True)
    grid_real = lax.dot_general(
        columns[0], cos_table, leading, preferred_element_type=jnp.float32
    ) + lax.dot_general(columns[1], sin_table, leading, preferred_element_type=jnp.float32)
    grid_imag = lax.dot_general(
        columns[1], cos_table, leading, preferred_element_type=jnp.float32
    ) - lax.dot_general(columns[0], sin_table, leading, preferred_element_type=jnp.float32)
    model = jnp.stack(
        [gains * grid_real.reshape(-1)[places], gains * grid_imag.reshape(-1)[places]]
    )
    fresh_dual = (dual + (model - seen)) / 2.0
    weighted = gains[None, :] * fresh_dual
    cell_count = grid_real.size
    hold_real = (
        jnp.zeros((cell_count,), jnp.float32)
        .at[places]
        .add(weighted[0])
        .reshape(grid_real.shape)
        .astype(jnp.bfloat16)
    )
    hold_imag = (
        jnp.zeros((cell_count,), jnp.float32)
        .at[places]
        .add(weighted[1])
        .reshape(grid_real.shape)
        .astype(jnp.bfloat16)
    )
    backward = jnp.stack(
        [
            jnp.dot(hold_real, cos_table, preferred_element_type=jnp.float32)
            - jnp.dot(hold_imag, sin_table, preferred_element_type=jnp.float32),
            jnp.dot(hold_real, sin_table, preferred_element_type=jnp.float32)
            + jnp.dot(hold_imag, cos_table, preferred_element_type=jnp.float32),
        ]
    ).astype(jnp.bfloat16)
    returned = lax.all_to_all(backward, "slab", split_axis=2, concat_axis=1, tiled=True)
    data_term = lax.dot_general(
        returned[0], cos_table, leading, preferred_element_type=jnp.float32
    ) - lax.dot_general(returned[1], sin_table, leading, preferred_element_type=jnp.float32)
    return (data_term, fresh_dual)


def wave_part(lifted, row_map, mask):
    highest = lax.Precision.HIGHEST
    count = lifted.shape[0]
    extended = with_halo(lifted, (("slab", 0),), HALO) * mask
    filtered = column_forward(extended)
    coef = lax.dot_general(
        row_map, filtered, leading, precision=highest, preferred_element_type=jnp.float32
    )
    squares = coef * coef
    share = lax.psum_scatter(
        squares.astype(jnp.bfloat16), "chan", scatter_dimension=1, tiled=True
    ).astype(jnp.float32)
    partial_factor = bound_level / jnp.maximum(jnp.sqrt(share), bound_level)
    factor = lax.all_gather(partial_factor, "chan", axis=1, tiled=True)
    fresh_dual = coef * factor
    back = column_adjoint(fresh_dual)
    spread = jnp.dot(row_map, back, precision=highest, preferred_element_type=jnp.float32) * mask
    bands = jnp.concatenate([spread[:HALO], spread[count + HALO :]], axis=0)
    arrived = with_halo(bands, (("slab", 0),), HALO)
    inner = spread[HALO : count + HALO]
    inner = inner.at[:HALO].add(arrived[:HALO])
    inner = inner.at[count - HALO :].add(arrived[3 * HALO :])
    return (inner, fresh_dual)


def local_plain(image, margin, cells, weights, observed, dual_start):
    count = image.shape[1]
    cos_table, sin_table = fourier_tables(N)
    row_map = row_matrix(count)
    mask = facet_mask(count, margin)[0][:, None]
    places = cells[0]
    gains = weights[0]
    seen = observed[:, 0, :]
    dual = dual_start[:, 0, :]
    estimate = image[0]
    data_term, dual = data_part(estimate, dual, seen, places, gains, cos_table, sin_table)
    wave_term, wave_dual = wave_part(estimate, row_map, mask)
    fresh = jnp.maximum(estimate - tau_step * (data_term + wave_term), 0.0)
    return (fresh[None], dual[:, None, :])


LANES = 128
EDGE = 8
CHUNK = 512
highest = lax.Precision.HIGHEST
crossed = (((1,), (1,)), ((), ()))


def pick(offset, taps):
    inside = (offset >= 0) & (offset < 8)
    return np.where(inside, np.asarray(taps, np.float64)[np.clip(offset, 0, 7)], 0.0)


def both_taps(offset, is_low):
    return np.where(is_low, pick(offset, low_taps), pick(offset, high_taps)).astype(np.float32)


def base_tables(length):
    index = np.arange(length)[:, None] * np.arange(LANES)[None, :] % length
    angle = index * (2.0 * np.pi / length)
    scale = 1.0 / np.sqrt(length)
    return np.stack([np.cos(angle) * scale, np.sin(angle) * scale]).astype(np.float32)


def turn_tables(length):
    blocks = length // LANES
    turns = np.arange(blocks)[:, None] * np.arange(blocks)[None, :] % blocks
    angle = turns * (2.0 * np.pi / blocks)
    values = np.stack([np.cos(angle), np.sin(angle)])[..., None]
    return np.broadcast_to(values, (2, blocks, blocks, LANES)).astype(np.float32)


def analysis_map():
    line = np.arange(4 * LANES)[:, None]
    column = np.arange(2 * LANES)[None, :]
    offset = line - (LANES - HALO) - 2 * (column % LANES)
    return both_taps(offset, column < LANES)


def synthesis_map():
    line = np.arange(6 * LANES)[:, None]
    column = np.arange(2 * LANES)[None, :]
    block = line // (2 * LANES) - 1
    offset = column - 2 * LANES * block - 2 * (line % LANES) + HALO
    return both_taps(offset, line % (2 * LANES) < LANES)


def wide_row_map(count):
    half = count // 2
    line = np.arange(count + 2 * EDGE)[:, None] - (EDGE - HALO)
    column = np.arange(count)[None, :]
    offset = line - 2 * (column % half)
    return both_taps(offset, column < half)


def whole_kernel(
    n, c, img, margin, cells, gains, seen, dual, base, turn, m1, m2, rows, rows_t, out, vout,
    tc, ts, hot, send1, recv1, send2, recv2, padded, halo, coef, sq, sq_in, cpad, spread, bands,
    grid_hi, grid_lo, marks, hold,
    sa, ra, sb, rb, sh, rh, ss, rs, sd, rd,
):
    me = lax.axis_index("slab")
    ch = lax.axis_index("chan")
    count, width = img.shape
    blocks = width // LANES
    vis = cells.shape[1]
    after, before = lax.rem(me + 1, n), lax.rem(me + n - 1, n)

    barrier = pltpu.get_barrier_semaphore()
    for d in range(1, n):
        pl.semaphore_signal(
            barrier, inc=1, device_id={"slab": lax.rem(me + d, n)},
            device_id_type=pl.DeviceIdType.MESH,
        )
    for d in range(1, c):
        pl.semaphore_signal(
            barrier, inc=1, device_id={"chan": lax.rem(ch + d, c)},
            device_id_type=pl.DeviceIdType.MESH,
        )

    def remote(src, dst, s, r, where):
        return pltpu.make_async_remote_copy(
            src_ref=src, dst_ref=dst, send_sem=s, recv_sem=r, device_id=where,
            device_id_type=pl.DeviceIdType.MESH,
        )

    base_c = base[0].reshape(width // 8, 8, LANES)
    base_s = base[1].reshape(width // 8, 8, LANES)
    for b in range(blocks):
        kc, ks = turn[0, b][None], turn[1, b][None]
        here = slice(b * LANES, (b + 1) * LANES)
        tc[:, here] = (base_c * kc - base_s * ks).reshape(width, LANES).astype(jnp.bfloat16)
        ts[:, here] = (base_s * kc + base_c * ks).reshape(width, LANES).astype(jnp.bfloat16)

    flat_b = img[...].astype(jnp.bfloat16)
    spec = lax.dot_general(tc[...], flat_b, crossed, preferred_element_type=jnp.float32)
    send1[:, :count, :] = spec.astype(jnp.bfloat16).reshape(n, count, count)
    spec = lax.dot_general(ts[...], flat_b, crossed, preferred_element_type=jnp.float32)
    send1[:, count:, :] = (-spec).astype(jnp.bfloat16).reshape(n, count, count)

    pl.semaphore_wait(barrier, n + c - 2)
    up = remote(img.at[count - EDGE :], halo.at[0], sh.at[0], rh.at[0], {"slab": after})
    down = remote(img.at[:EDGE], halo.at[1], sh.at[1], rh.at[1], {"slab": before})
    up.start()
    down.start()
    sends1 = []
    for d in range(1, n):
        peer = lax.rem(me + d, n)
        copy = remote(send1.at[peer], recv1.at[me], sa.at[d], ra.at[me], {"slab": peer})
        copy.start()
        sends1.append(copy)
    recv1[me] = send1[me]

    spot = cells[...]
    low_spot = spot % width
    step = 32

    def make_hot(i, carry):
        line = lax.broadcasted_iota(jnp.int32, (step, vis), 0) + i * step
        hit = jnp.where(line == low_spot, 1.0, 0.0).astype(jnp.bfloat16)
        hot[pl.ds(pl.multiple_of(i * step, step), step), :] = hit
        return carry

    lax.fori_loop(0, width // step, make_hot, 0)

    reach = margin[0]
    tall = count + 2 * EDGE

    def keep(shape, dim):
        line = lax.broadcasted_iota(jnp.int32, shape, dim)
        distance = jnp.maximum(jnp.maximum(EDGE - line, line - count - EDGE + 1), 0)
        return jnp.where(distance <= reach, 1.0, 0.0)

    row_fwd = rows_t[...] * keep((count, tall), 1)
    row_adj = rows[...] * keep((tall, count), 0)

    padded[:, :LANES] = jnp.zeros((tall, LANES), jnp.float32)
    padded[:, LANES + width :] = jnp.zeros((tall, LANES), jnp.float32)
    padded[EDGE : EDGE + count, LANES : LANES + width] = img[...]
    up.wait_recv()
    down.wait_recv()
    padded[:EDGE, LANES : LANES + width] = jnp.where(me > 0, halo[0], 0.0)
    padded[EDGE + count :, LANES : LANES + width] = jnp.where(me < n - 1, halo[1], 0.0)
    pair = 2 * LANES
    for b in range(width // pair):
        filtered = jnp.dot(
            padded[:, b * pair : b * pair + 4 * LANES], m1[...], precision=highest,
            preferred_element_type=jnp.float32,
        )
        part = jnp.dot(row_fwd, filtered, precision=highest, preferred_element_type=jnp.float32)
        coef[:, b * pair : (b + 1) * pair] = part
        sq[:, b * pair : (b + 1) * pair] = (part * part).astype(jnp.bfloat16)
    sends_q = []
    for d in range(1, c):
        peer = lax.rem(ch + d, c)
        copy = remote(sq, sq_in.at[ch], ss.at[d], rs.at[ch], {"chan": peer})
        copy.start()
        sends_q.append(copy)
    sq_in[ch] = sq[...]

    for d in range(1, n):
        src = lax.rem(me + d, n)
        remote(send1.at[src], recv1.at[src], sa.at[d], ra.at[src], {"slab": src}).wait_recv()
    columns = jnp.concatenate([recv1[j] for j in range(n)], axis=1)
    by_cos = jnp.dot(columns, tc[...], preferred_element_type=jnp.float32)
    by_sin = jnp.dot(columns, ts[...], preferred_element_type=jnp.float32)
    grid = jnp.concatenate(
        [by_cos[:count] + by_sin[count:], by_cos[count:] - by_sin[:count]], axis=0
    )
    hi = grid.astype(jnp.bfloat16)
    grid_hi[...] = hi
    grid_lo[...] = (grid - hi.astype(jnp.float32)).astype(jnp.bfloat16)

    def visit(i, carry):
        here = pl.ds(pl.multiple_of(i * CHUNK, CHUNK), CHUNK)
        table = hot[:, here]
        found = jnp.dot(grid_hi[...], table, preferred_element_type=jnp.float32)
        found = found + jnp.dot(grid_lo[...], table, preferred_element_type=jnp.float32)
        line = lax.broadcasted_iota(jnp.int32, (count, CHUNK), 0)
        match = line == cells[:, here] // width
        gain = gains[:, here]
        for part in range(2):
            mine = found[part * count : (part + 1) * count]
            value = jnp.sum(jnp.where(match, mine, 0.0), axis=0, keepdims=True)
            fresh = (dual[part, :, here] + (gain * value - seen[part, :, here])) / 2.0
            vout[part, :, here] = fresh
            marks[part * count : (part + 1) * count, here] = jnp.where(
                match, gain * fresh, 0.0
            ).astype(jnp.bfloat16)
        return carry

    lax.fori_loop(0, vis // CHUNK, visit, 0)

    def collect(i, carry):
        here = pl.ds(pl.multiple_of(i * pair, pair), pair)
        hold[here, :] = lax.dot_general(
            hot[here, :], marks[...], crossed, preferred_element_type=jnp.float32
        ).astype(jnp.bfloat16)
        return carry

    lax.fori_loop(0, width // pair, collect, 0)

    sends2 = []
    for d in range(1, n + 1):
        peer = lax.rem(me + d, n)
        here = pl.ds(pl.multiple_of(peer * count, count), count)
        by_cos = jnp.dot(tc[here, :], hold[...], preferred_element_type=jnp.float32)
        by_sin = jnp.dot(ts[here, :], hold[...], preferred_element_type=jnp.float32)
        real = (by_cos[:, :count] - by_sin[:, count:]).astype(jnp.bfloat16)
        imag = (by_sin[:, :count] + by_cos[:, count:]).astype(jnp.bfloat16)
        if d < n:
            send2[peer, :, :count] = real
            send2[peer, :, count:] = imag
            copy = remote(send2.at[peer], recv2.at[me], sb.at[d], rb.at[me], {"slab": peer})
            copy.start()
            sends2.append(copy)
        else:
            recv2[me, :, :count] = real
            recv2[me, :, count:] = imag

    for d in range(1, c):
        src = lax.rem(ch + d, c)
        remote(sq, sq_in.at[src], ss.at[d], rs.at[src], {"chan": src}).wait_recv()
    cpad[:, :pair] = jnp.zeros((count, pair), jnp.float32)
    cpad[:, pair + width :] = jnp.zeros((count, pair), jnp.float32)
    for b in range(width // pair):
        here = slice(b * pair, (b + 1) * pair)
        total = sq_in[0, :, here].astype(jnp.float32)
        for j in range(1, c):
            total = total + sq_in[j, :, here].astype(jnp.float32)
        factor = bound_level / jnp.maximum(jnp.sqrt(total), bound_level)
        cpad[:, (b + 1) * pair : (b + 2) * pair] = coef[:, here] * factor
    for b in range(width // pair):
        back = jnp.dot(
            cpad[:, b * pair : b * pair + 6 * LANES], m2[...], precision=highest,
            preferred_element_type=jnp.float32,
        )
        spread[:, b * pair : (b + 1) * pair] = jnp.dot(
            row_adj, back, precision=highest, preferred_element_type=jnp.float32
        )
    over = remote(spread.at[count + EDGE :], bands.at[0], sd.at[0], rd.at[0], {"slab": after})
    under = remote(spread.at[:EDGE], bands.at[1], sd.at[1], rd.at[1], {"slab": before})
    over.start()
    under.start()
    over.wait_recv()
    under.wait_recv()
    wave_first = spread[EDGE : 2 * EDGE, :] + jnp.where(me > 0, bands[0], 0.0)
    wave_last = spread[count : count + EDGE, :] + jnp.where(me < n - 1, bands[1], 0.0)
    wave = jnp.concatenate(
        [wave_first, spread[2 * EDGE : count, :], wave_last], axis=0
    )

    for d in range(1, n):
        src = lax.rem(me + d, n)
        remote(send2.at[src], recv2.at[src], sb.at[d], rb.at[src], {"slab": src}).wait_recv()
    real = jnp.concatenate([recv2[j, :, :count] for j in range(n)], axis=1)
    imag = jnp.concatenate([recv2[j, :, count:] for j in range(n)], axis=1)
    term = jnp.dot(real, tc[...], preferred_element_type=jnp.float32)
    term = term - jnp.dot(imag, ts[...], preferred_element_type=jnp.float32)
    out[...] = jnp.maximum(img[...] - tau_step * (term + wave), 0.0)

    for copy in [up, down, over, under] + sends1 + sends_q + sends2:
        copy.wait_send()


def local_kernel(n, c, image, margin, cells, weights, observed, dual_start):
    count, width = image.shape[1], image.shape[2]
    vis = cells.shape[1]
    tall = count + 2 * EDGE
    half_t, f32 = jnp.bfloat16, jnp.float32
    V = pltpu.VMEM
    dma = pltpu.SemaphoreType.DMA
    row_map = wide_row_map(count)
    vm = pl.BlockSpec(memory_space=pltpu.VMEM)
    fresh, dual = pl.pallas_call(
        functools.partial(whole_kernel, n, c),
        out_shape=(
            jax.ShapeDtypeStruct((count, width), f32),
            jax.ShapeDtypeStruct((2, 1, vis), f32),
        ),
        in_specs=[vm, pl.BlockSpec(memory_space=pltpu.SMEM)] + [vm] * 10,
        out_specs=(vm, vm),
        scratch_shapes=[
            V((width, width), half_t),
            V((width, width), half_t),
            V((width, vis), half_t),
            V((n, 2 * count, count), half_t),
            V((n, 2 * count, count), half_t),
            V((n, count, 2 * count), half_t),
            V((n, count, 2 * count), half_t),
            V((tall, width + 2 * LANES), f32),
            V((2, EDGE, width), f32),
            V((count, width), f32),
            V((count, width), half_t),
            V((c, count, width), half_t),
            V((count, width + 4 * LANES), f32),
            V((tall, width), f32),
            V((2, EDGE, width), f32),
            V((2 * count, width), half_t),
            V((2 * count, width), half_t),
            V((2 * count, vis), half_t),
            V((width, 2 * count), half_t),
            dma((n,)), dma((n,)), dma((n,)), dma((n,)), dma((2,)), dma((2,)),
            dma((c,)), dma((c,)), dma((2,)), dma((2,)),
        ],
        compiler_params=pltpu.CompilerParams(
            collective_id=0, has_side_effects=True, vmem_limit_bytes=60 * 1024 * 1024
        ),
    )(
        image[0], margin, cells, weights, observed, dual_start,
        base_tables(width), turn_tables(width), analysis_map(), synthesis_map(),
        row_map, np.ascontiguousarray(row_map.T),
    )
    return (fresh[None], dual)


def solution(mesh):
    n, c = mesh.shape["slab"], mesh.shape["chan"]

    def local(image, *rest):
        count, width = image.shape[1], image.shape[2]
        if count == LANES and width == 8 * LANES and rest[1].shape[1] % CHUNK == 0:
            return local_kernel(n, c, image, *rest)
        return local_plain(image, *rest)

    in_specs = (
        P("chan", "slab", None),
        P("slab"),
        P("chan", "slab"),
        P("chan", "slab"),
        P(None, "chan", "slab"),
        P(None, "chan", "slab"),
    )
    out_specs = (P("chan", "slab", None), P(None, "chan", "slab"))
    return jax.shard_map(local, mesh=mesh, in_specs=in_specs, out_specs=out_specs, check_vma=False)
```

```python
import functools
import math

import jax
import jax.numpy as jnp
import numpy as np
from jax import lax
from jax.experimental import pallas as pl
from jax.experimental.pallas import tpu as pltpu
from jax.sharding import PartitionSpec as P

N = 1024
HALO = 3


low_taps = (
    -0.010597401784997278,
    0.032883011666982945,
    0.030841381835986965,
    -0.18703481171888114,
    -0.02798376941698385,
    0.6308807679295904,
    0.7148465705525415,
    0.23037781330885523,
)
high_taps = (
    -0.23037781330885523,
    0.7148465705525415,
    -0.6308807679295904,
    -0.02798376941698385,
    0.18703481171888114,
    0.030841381835986965,
    -0.032883011666982945,
    -0.010597401784997278,
)
tau_step = 0.5
bound_level = 3.0
leading = (((0,), (0,)), ((), ()))


def with_halo(block, sides, width):
    for axis, dim in sides:
        count = lax.axis_size(axis)
        forward = [(i, i + 1) for i in range(count - 1)]
        backward = [(target, source) for source, target in forward]
        low = lax.ppermute(
            lax.slice_in_dim(block, block.shape[dim] - width, None, axis=dim), axis, forward
        )
        high = lax.ppermute(lax.slice_in_dim(block, 0, width, axis=dim), axis, backward)
        block = jnp.concatenate([low, block, high], axis=dim)
    return block


def tap_value(offset, taps):
    total = jnp.zeros(offset.shape, jnp.float32)
    for position in range(8):
        total = total + jnp.where(offset == position, taps[position], 0.0).astype(jnp.float32)
    return total


def fourier_tables(length):
    index = jnp.arange(length, dtype=jnp.int32)
    product = index[:, None] * index[None, :] % length
    angle = product.astype(jnp.float32) * (2.0 * math.pi / length)
    scale = 1.0 / math.sqrt(length)
    return (
        (jnp.cos(angle) * scale).astype(jnp.bfloat16),
        (jnp.sin(angle) * scale).astype(jnp.bfloat16),
    )


def row_matrix(count):
    half = count // 2
    line = jnp.arange(count + 2 * HALO, dtype=jnp.int32)[:, None]
    column = jnp.arange(count, dtype=jnp.int32)[None, :]
    offset = line - 2 * (column % half)
    return jnp.where(column < half, tap_value(offset, low_taps), tap_value(offset, high_taps))


def facet_mask(count, width):
    line = jnp.arange(count + 2 * HALO, dtype=jnp.int32)
    distance = jnp.maximum(jnp.maximum(HALO - line, line - count - HALO + 1), 0)
    return (distance[None, :] <= width[:, None]).astype(jnp.float32)


def column_forward(values):
    width = values.shape[1]
    half = width // 2
    padded = jnp.pad(values, ((0, 0), (HALO, 8)))
    even_cells = padded[:, 0::2]
    odd_cells = padded[:, 1::2]
    low_part = jnp.zeros((values.shape[0], half), jnp.float32)
    high_part = jnp.zeros((values.shape[0], half), jnp.float32)
    for position in range(8):
        source = even_cells if position % 2 == 0 else odd_cells
        piece = source[:, position // 2 : position // 2 + half]
        low_part = low_part + low_taps[position] * piece
        high_part = high_part + high_taps[position] * piece
    return jnp.concatenate([low_part, high_part], axis=1)


def column_adjoint(coefs):
    width = coefs.shape[1]
    half = width // 2
    low_part = coefs[:, :half]
    high_part = coefs[:, half:]
    even_sums = jnp.zeros((coefs.shape[0], half + 4), jnp.float32)
    odd_sums = jnp.zeros((coefs.shape[0], half + 4), jnp.float32)
    for position in range(8):
        term = low_taps[position] * low_part + high_taps[position] * high_part
        placed = jnp.pad(term, ((0, 0), (position // 2, 4 - position // 2)))
        if position % 2 == 0:
            even_sums = even_sums + placed
        else:
            odd_sums = odd_sums + placed
    joined = jnp.stack([even_sums, odd_sums], axis=2).reshape(coefs.shape[0], width + 8)
    return joined[:, HALO : HALO + width]


def data_part(lifted, dual, seen, places, gains, cos_table, sin_table):
    flat_b = lifted.astype(jnp.bfloat16)
    spectra = jnp.stack(
        [
            jnp.dot(flat_b, cos_table, preferred_element_type=jnp.float32),
            -jnp.dot(flat_b, sin_table, preferred_element_type=jnp.float32),
        ]
    ).astype(jnp.bfloat16)
    columns = lax.all_to_all(spectra, "slab", split_axis=2, concat_axis=1, tiled=True)
    grid_real = lax.dot_general(
        columns[0], cos_table, leading, preferred_element_type=jnp.float32
    ) + lax.dot_general(columns[1], sin_table, leading, preferred_element_type=jnp.float32)
    grid_imag = lax.dot_general(
        columns[1], cos_table, leading, preferred_element_type=jnp.float32
    ) - lax.dot_general(columns[0], sin_table, leading, preferred_element_type=jnp.float32)
    model = jnp.stack(
        [gains * grid_real.reshape(-1)[places], gains * grid_imag.reshape(-1)[places]]
    )
    fresh_dual = (dual + (model - seen)) / 2.0
    weighted = gains[None, :] * fresh_dual
    cell_count = grid_real.size
    hold_real = (
        jnp.zeros((cell_count,), jnp.float32)
        .at[places]
        .add(weighted[0])
        .reshape(grid_real.shape)
        .astype(jnp.bfloat16)
    )
    hold_imag = (
        jnp.zeros((cell_count,), jnp.float32)
        .at[places]
        .add(weighted[1])
        .reshape(grid_real.shape)
        .astype(jnp.bfloat16)
    )
    backward = jnp.stack(
        [
            jnp.dot(hold_real, cos_table, preferred_element_type=jnp.float32)
            - jnp.dot(hold_imag, sin_table, preferred_element_type=jnp.float32),
            jnp.dot(hold_real, sin_table, preferred_element_type=jnp.float32)
            + jnp.dot(hold_imag, cos_table, preferred_element_type=jnp.float32),
        ]
    ).astype(jnp.bfloat16)
    returned = lax.all_to_all(backward, "slab", split_axis=2, concat_axis=1, tiled=True)
    data_term = lax.dot_general(
        returned[0], cos_table, leading, preferred_element_type=jnp.float32
    ) - lax.dot_general(returned[1], sin_table, leading, preferred_element_type=jnp.float32)
    return (data_term, fresh_dual)


def wave_part(lifted, row_map, mask):
    highest = lax.Precision.HIGHEST
    count = lifted.shape[0]
    extended = with_halo(lifted, (("slab", 0),), HALO) * mask
    filtered = column_forward(extended)
    coef = lax.dot_general(
        row_map, filtered, leading, precision=highest, preferred_element_type=jnp.float32
    )
    squares = coef * coef
    share = lax.psum_scatter(
        squares.astype(jnp.bfloat16), "chan", scatter_dimension=1, tiled=True
    ).astype(jnp.float32)
    partial_factor = bound_level / jnp.maximum(jnp.sqrt(share), bound_level)
    factor = lax.all_gather(partial_factor, "chan", axis=1, tiled=True)
    fresh_dual = coef * factor
    back = column_adjoint(fresh_dual)
    spread = jnp.dot(row_map, back, precision=highest, preferred_element_type=jnp.float32) * mask
    bands = jnp.concatenate([spread[:HALO], spread[count + HALO :]], axis=0)
    arrived = with_halo(bands, (("slab", 0),), HALO)
    inner = spread[HALO : count + HALO]
    inner = inner.at[:HALO].add(arrived[:HALO])
    inner = inner.at[count - HALO :].add(arrived[3 * HALO :])
    return (inner, fresh_dual)


def local_plain(image, margin, cells, weights, observed, dual_start):
    count = image.shape[1]
    cos_table, sin_table = fourier_tables(N)
    row_map = row_matrix(count)
    mask = facet_mask(count, margin)[0][:, None]
    places = cells[0]
    gains = weights[0]
    seen = observed[:, 0, :]
    dual = dual_start[:, 0, :]
    estimate = image[0]
    data_term, dual = data_part(estimate, dual, seen, places, gains, cos_table, sin_table)
    wave_term, wave_dual = wave_part(estimate, row_map, mask)
    fresh = jnp.maximum(estimate - tau_step * (data_term + wave_term), 0.0)
    return (fresh[None], dual[:, None, :])


LANES = 128
EDGE = 8
CHUNK = 512
highest = lax.Precision.HIGHEST
crossed = (((1,), (1,)), ((), ()))


def pick(offset, taps):
    inside = (offset >= 0) & (offset < 8)
    return np.where(inside, np.asarray(taps, np.float64)[np.clip(offset, 0, 7)], 0.0)


def both_taps(offset, is_low):
    return np.where(is_low, pick(offset, low_taps), pick(offset, high_taps)).astype(np.float32)


def base_tables(length):
    index = np.arange(length)[:, None] * np.arange(LANES)[None, :] % length
    angle = index * (2.0 * np.pi / length)
    scale = 1.0 / np.sqrt(length)
    return np.stack([np.cos(angle) * scale, np.sin(angle) * scale]).astype(np.float32)


def turn_tables(length):
    blocks = length // LANES
    turns = np.arange(blocks)[:, None] * np.arange(blocks)[None, :] % blocks
    angle = turns * (2.0 * np.pi / blocks)
    values = np.stack([np.cos(angle), np.sin(angle)])[..., None]
    return np.broadcast_to(values, (2, blocks, blocks, LANES)).astype(np.float32)


def analysis_map():
    line = np.arange(4 * LANES)[:, None]
    column = np.arange(2 * LANES)[None, :]
    offset = line - (LANES - HALO) - 2 * (column % LANES)
    return both_taps(offset, column < LANES)


def synthesis_map():
    line = np.arange(6 * LANES)[:, None]
    column = np.arange(2 * LANES)[None, :]
    block = line // (2 * LANES) - 1
    offset = column - 2 * LANES * block - 2 * (line % LANES) + HALO
    return both_taps(offset, line % (2 * LANES) < LANES)


def wide_row_map(count):
    half = count // 2
    line = np.arange(count + 2 * EDGE)[:, None] - (EDGE - HALO)
    column = np.arange(count)[None, :]
    offset = line - 2 * (column % half)
    return both_taps(offset, column < half)


def in_two(values):
    top = values.astype(jnp.bfloat16)
    return np.stack([top, (values - top.astype(np.float32)).astype(jnp.bfloat16)])


def split(value):
    top = value.astype(jnp.bfloat16)
    return top, (value - top.astype(jnp.float32)).astype(jnp.bfloat16)


def fine_dot(left, right):
    total = jnp.dot(left[0], right[0], preferred_element_type=jnp.float32)
    total = total + jnp.dot(left[1], right[0], preferred_element_type=jnp.float32)
    return total + jnp.dot(left[0], right[1], preferred_element_type=jnp.float32)


def flip(place, bits):
    result = place
    for bit in (1, 2, 4):
        if bits & bit:
            result = result + bit - 2 * bit * (place // bit % 2)
    return result


def whole_kernel(
    n, c, img, margin, cells, gains, seen, dual, base, turn, m1_far, m2_far, rows_far, rows_t_far,
    out, vout, m1, m2, rows, rows_t, fetched, found_half,
    tc, ts, hot, send1, recv1, send2, recv2, padded, halo, coef, sq, sq_in, cpad, spread, bands,
    grid, marks, hold, u_spot,
    sa, ra, sb, rb, sh, rh, ss, rs, sd, rd,
):
    me = lax.axis_index("slab")
    ch = lax.axis_index("chan")
    count, width = img.shape
    blocks = width // LANES
    vis = cells.shape[1]
    after, before = lax.rem(me + 1, n), lax.rem(me + n - 1, n)

    barrier = pltpu.get_barrier_semaphore()
    for d in range(1, n):
        pl.semaphore_signal(
            barrier, inc=1, device_id={"slab": lax.rem(me + d, n)},
            device_id_type=pl.DeviceIdType.MESH,
        )
    for d in range(1, c):
        pl.semaphore_signal(
            barrier, inc=1, device_id={"chan": lax.rem(ch + d, c)},
            device_id_type=pl.DeviceIdType.MESH,
        )

    def remote(src, dst, s, r, where):
        return pltpu.make_async_remote_copy(
            src_ref=src, dst_ref=dst, send_sem=s, recv_sem=r, device_id=where,
            device_id_type=pl.DeviceIdType.MESH,
        )

    fetches = [
        pltpu.make_async_copy(far, near, fetched.at[i])
        for i, (far, near) in enumerate(
            [(m1_far, m1), (rows_far, rows), (rows_t_far, rows_t), (m2_far, m2)]
        )
    ]
    for fetch in fetches:
        fetch.start()

    base_c = base[0].reshape(width // 8, 8, LANES)
    base_s = base[1].reshape(width // 8, 8, LANES)
    for b in range(blocks):
        kc, ks = turn[0, b][None], turn[1, b][None]
        here = slice(b * LANES, (b + 1) * LANES)
        tc[:, here] = (base_c * kc - base_s * ks).reshape(width, LANES).astype(jnp.bfloat16)
        ts[:, here] = (base_s * kc + base_c * ks).reshape(width, LANES).astype(jnp.bfloat16)

    flat_b = img[...].astype(jnp.bfloat16)
    part = count // 2
    spec = lax.dot_general(tc[...], flat_b, crossed, preferred_element_type=jnp.float32)
    send1[:, :, :part, :] = spec.astype(jnp.bfloat16).reshape(n, 2, part, count)
    spec = lax.dot_general(ts[...], flat_b, crossed, preferred_element_type=jnp.float32)
    send1[:, :, part:, :] = (-spec).astype(jnp.bfloat16).reshape(n, 2, part, count)

    pl.semaphore_wait(barrier, n + c - 2)
    up = remote(img.at[count - EDGE :], halo.at[0], sh.at[0], rh.at[0], {"slab": after})
    down = remote(img.at[:EDGE], halo.at[1], sh.at[1], rh.at[1], {"slab": before})
    up.start()
    down.start()
    sends1 = []
    for h in range(2):
        for d in range(n - 1, 0, -1):
            peer = flip(me, d)
            copy = remote(
                send1.at[peer, h], recv1.at[me, h], sa.at[h, d], ra.at[h, me], {"slab": peer}
            )
            copy.start()
            sends1.append(copy)
    recv1[me] = send1[me]

    spot = cells[...]
    low_spot = spot % width
    step = 32

    def make_hot(i, carry):
        line = lax.broadcasted_iota(jnp.int32, (step, vis), 0) + i * step
        hit = jnp.where(line == low_spot, 1.0, 0.0).astype(jnp.bfloat16)
        hot[pl.ds(pl.multiple_of(i * step, step), step), :] = hit
        return carry

    lax.fori_loop(0, width // step, make_hot, 0)

    reach = margin[0]
    tall = count + 2 * EDGE

    def keep(shape, dim):
        line = lax.broadcasted_iota(jnp.int32, shape, dim)
        distance = jnp.maximum(jnp.maximum(EDGE - line, line - count - EDGE + 1), 0)
        return jnp.where(distance <= reach, 1.0, 0.0)

    for fetch in fetches:
        fetch.wait()
    row_fwd = split(rows_t[...] * keep((count, tall), 1))
    row_adj = split(rows[...] * keep((tall, count), 0))

    padded[:, :LANES] = jnp.zeros((tall, LANES), jnp.float32)
    padded[:, LANES + width :] = jnp.zeros((tall, LANES), jnp.float32)
    padded[EDGE : EDGE + count, LANES : LANES + width] = img[...]
    up.wait_recv()
    down.wait_recv()
    padded[:EDGE, LANES : LANES + width] = jnp.where(me > 0, halo[0], 0.0)
    padded[EDGE + count :, LANES : LANES + width] = jnp.where(me < n - 1, halo[1], 0.0)
    pair = 2 * LANES
    for b in range(width // pair):
        filtered = fine_dot(split(padded[:, b * pair : b * pair + 4 * LANES]), m1)
        piece = fine_dot(row_fwd, split(filtered))
        coef[:, b * pair : (b + 1) * pair] = piece
        sq[:, b * pair : (b + 1) * pair] = (piece * piece).astype(jnp.bfloat16)
    sends_q = []
    for d in range(1, c):
        peer = lax.rem(ch + d, c)
        copy = remote(sq, sq_in.at[ch], ss.at[d], rs.at[ch], {"chan": peer})
        copy.start()
        sends_q.append(copy)
    sq_in[ch] = sq[...]

    u_spot[...] = spot // width

    def look(h, here):
        found = jnp.dot(grid[h], hot[:, here], preferred_element_type=jnp.float32)
        found = found[:count] + found[count:]
        line = lax.broadcasted_iota(jnp.int32, (part, CHUNK), 0) + h * part
        match = line == u_spot[:, here]
        return [
            jnp.sum(
                jnp.where(match, found[k * part : (k + 1) * part], 0.0), axis=0, keepdims=True
            )
            for k in range(2)
        ]

    def visit_first(i, carry):
        here = pl.ds(pl.multiple_of(i * CHUNK, CHUNK), CHUNK)
        values = look(0, here)
        for k in range(2):
            found_half[k, :, here] = values[k]
        return carry

    def visit_last(i, carry):
        here = pl.ds(pl.multiple_of(i * CHUNK, CHUNK), CHUNK)
        values = look(1, here)
        line = lax.broadcasted_iota(jnp.int32, (count, CHUNK), 0)
        match = line == u_spot[:, here]
        gain = gains[:, here]
        for k in range(2):
            value = values[k] + found_half[k, :, here]
            fresh = (dual[k, :, here] + (gain * value - seen[k, :, here])) / 2.0
            vout[k, :, here] = fresh
            marks[k * count : (k + 1) * count, here] = jnp.where(
                match, gain * fresh, 0.0
            ).astype(jnp.bfloat16)
        return carry

    for h in range(2):
        for d in range(n - 1, 0, -1):
            src = flip(me, d)
            remote(
                send1.at[src, h], recv1.at[src, h], sa.at[h, d], ra.at[h, src], {"slab": src}
            ).wait_recv()
        columns = jnp.concatenate([recv1[j, h] for j in range(n)], axis=1)
        by_cos = jnp.dot(columns, tc[...], preferred_element_type=jnp.float32)
        by_sin = jnp.dot(columns, ts[...], preferred_element_type=jnp.float32)
        values = jnp.concatenate(
            [by_cos[:part] + by_sin[part:], by_cos[part:] - by_sin[:part]], axis=0
        )
        grid[h] = jnp.concatenate(split(values), axis=0)
        lax.fori_loop(0, vis // CHUNK, (visit_first, visit_last)[h], 0, unroll=2)

    hold[...] = lax.dot_general(
        hot[...], marks[...], crossed, preferred_element_type=jnp.float32
    ).astype(jnp.bfloat16)

    sends2 = []
    for d in range(n - 1, -1, -1):
        peer = flip(me, d)
        here = pl.ds(pl.multiple_of(peer * count, count), count)
        by_cos = jnp.dot(tc[here, :], hold[...], preferred_element_type=jnp.float32)
        by_sin = jnp.dot(ts[here, :], hold[...], preferred_element_type=jnp.float32)
        real = (by_cos[:, :count] - by_sin[:, count:]).astype(jnp.bfloat16)
        imag = (by_sin[:, :count] + by_cos[:, count:]).astype(jnp.bfloat16)
        if d > 0:
            send2[peer, :, :count] = real
            send2[peer, :, count:] = imag
            copy = remote(send2.at[peer], recv2.at[me], sb.at[d], rb.at[me], {"slab": peer})
            copy.start()
            sends2.append(copy)
        else:
            recv2[me, :, :count] = real
            recv2[me, :, count:] = imag

    for d in range(1, c):
        src = lax.rem(ch + d, c)
        remote(sq, sq_in.at[src], ss.at[d], rs.at[src], {"chan": src}).wait_recv()
    cpad[:, :pair] = jnp.zeros((count, pair), jnp.float32)
    cpad[:, pair + width :] = jnp.zeros((count, pair), jnp.float32)
    for b in range(width // pair):
        here = slice(b * pair, (b + 1) * pair)
        total = sq_in[0, :, here].astype(jnp.float32)
        for j in range(1, c):
            total = total + sq_in[j, :, here].astype(jnp.float32)
        factor = bound_level / jnp.maximum(jnp.sqrt(total), bound_level)
        cpad[:, (b + 1) * pair : (b + 2) * pair] = coef[:, here] * factor
    for b in range(width // pair):
        back = fine_dot(split(cpad[:, b * pair : b * pair + 6 * LANES]), m2)
        spread[:, b * pair : (b + 1) * pair] = fine_dot(row_adj, split(back))
    over = remote(spread.at[count + EDGE :], bands.at[0], sd.at[0], rd.at[0], {"slab": after})
    under = remote(spread.at[:EDGE], bands.at[1], sd.at[1], rd.at[1], {"slab": before})
    over.start()
    under.start()

    side = n // 2
    term = None
    for far in range(2):
        for d in range(1 - far, side):
            src = flip(me, d + far * side)
            remote(
                send2.at[src], recv2.at[src], sb.at[d + far * side], rb.at[src], {"slab": src}
            ).wait_recv()
        first = (me // side + far) % 2 * side
        real = jnp.concatenate([recv2[first + j, :, :count] for j in range(side)], axis=1)
        imag = jnp.concatenate([recv2[first + j, :, count:] for j in range(side)], axis=1)
        here = pl.ds(pl.multiple_of(first * count, count), side * count)
        more = jnp.dot(real, tc[here, :], preferred_element_type=jnp.float32)
        more = more - jnp.dot(imag, ts[here, :], preferred_element_type=jnp.float32)
        term = more if term is None else term + more
    over.wait_recv()
    under.wait_recv()
    wave_first = spread[EDGE : 2 * EDGE, :] + jnp.where(me > 0, bands[0], 0.0)
    wave_last = spread[count : count + EDGE, :] + jnp.where(me < n - 1, bands[1], 0.0)
    wave = jnp.concatenate(
        [wave_first, spread[2 * EDGE : count, :], wave_last], axis=0
    )
    out[...] = jnp.maximum(img[...] - tau_step * (term + wave), 0.0)

    for copy in [up, down, over, under] + sends1 + sends_q + sends2:
        copy.wait_send()


def local_kernel(n, c, image, margin, cells, weights, observed, dual_start):
    count, width = image.shape[1], image.shape[2]
    vis = cells.shape[1]
    tall = count + 2 * EDGE
    half_t, f32 = jnp.bfloat16, jnp.float32
    V = pltpu.VMEM
    dma = pltpu.SemaphoreType.DMA
    row_map = wide_row_map(count)
    vm = pl.BlockSpec(memory_space=pltpu.VMEM)
    fresh, dual = pl.pallas_call(
        functools.partial(whole_kernel, n, c),
        out_shape=(
            jax.ShapeDtypeStruct((count, width), f32),
            jax.ShapeDtypeStruct((2, 1, vis), f32),
        ),
        in_specs=[vm, pl.BlockSpec(memory_space=pltpu.SMEM)] + [vm] * 6
        + [pl.BlockSpec(memory_space=pl.ANY)] * 4,
        out_specs=(vm, vm),
        scratch_shapes=[
            V((2, 4 * LANES, 2 * LANES), half_t),
            V((2, 6 * LANES, 2 * LANES), half_t),
            V((tall, count), f32),
            V((count, tall), f32),
            dma((4,)),
            V((2, 1, vis), f32),
            V((width, width), half_t),
            V((width, width), half_t),
            V((width, vis), half_t),
            V((n, 2, count, count), half_t),
            V((n, 2, count, count), half_t),
            V((n, count, 2 * count), half_t),
            V((n, count, 2 * count), half_t),
            V((tall, width + 2 * LANES), f32),
            V((2, EDGE, width), f32),
            V((count, width), f32),
            V((count, width), half_t),
            V((c, count, width), half_t),
            V((count, width + 4 * LANES), f32),
            V((tall, width), f32),
            V((2, EDGE, width), f32),
            V((2, 2 * count, width), half_t),
            V((2 * count, vis), half_t),
            V((width, 2 * count), half_t),
            V((1, vis), jnp.int32),
            dma((2, n)), dma((2, n)), dma((n,)), dma((n,)), dma((2,)), dma((2,)),
            dma((c,)), dma((c,)), dma((2,)), dma((2,)),
        ],
        compiler_params=pltpu.CompilerParams(
            collective_id=0, has_side_effects=True, vmem_limit_bytes=40 * 1024 * 1024
        ),
    )(
        image[0], margin, cells, weights, observed, dual_start,
        base_tables(width), turn_tables(width), in_two(analysis_map()), in_two(synthesis_map()),
        row_map, np.ascontiguousarray(row_map.T),
    )
    return (fresh[None], dual)


def solution(mesh):
    n, c = mesh.shape["slab"], mesh.shape["chan"]

    def local(image, *rest):
        count, width = image.shape[1], image.shape[2]
        if n == 8 and count == LANES and width == n * count and rest[1].shape[1] % CHUNK == 0:
            return local_kernel(n, c, image, *rest)
        return local_plain(image, *rest)

    in_specs = (
        P("chan", "slab", None),
        P("slab"),
        P("chan", "slab"),
        P("chan", "slab"),
        P(None, "chan", "slab"),
        P(None, "chan", "slab"),
    )
    out_specs = (P("chan", "slab", None), P(None, "chan", "slab"))
    return jax.shard_map(local, mesh=mesh, in_specs=in_specs, out_specs=out_specs, check_vma=False)
```

```python
import functools
import math

import jax
import jax.numpy as jnp
import numpy as np
from jax import lax
from jax.experimental import pallas as pl
from jax.experimental.pallas import tpu as pltpu
from jax.sharding import PartitionSpec as P

N = 1024
HALO = 3


low_taps = (
    -0.010597401784997278,
    0.032883011666982945,
    0.030841381835986965,
    -0.18703481171888114,
    -0.02798376941698385,
    0.6308807679295904,
    0.7148465705525415,
    0.23037781330885523,
)
high_taps = (
    -0.23037781330885523,
    0.7148465705525415,
    -0.6308807679295904,
    -0.02798376941698385,
    0.18703481171888114,
    0.030841381835986965,
    -0.032883011666982945,
    -0.010597401784997278,
)
tau_step = 0.5
bound_level = 3.0
leading = (((0,), (0,)), ((), ()))


def with_halo(block, sides, width):
    for axis, dim in sides:
        count = lax.axis_size(axis)
        forward = [(i, i + 1) for i in range(count - 1)]
        backward = [(target, source) for source, target in forward]
        low = lax.ppermute(
            lax.slice_in_dim(block, block.shape[dim] - width, None, axis=dim), axis, forward
        )
        high = lax.ppermute(lax.slice_in_dim(block, 0, width, axis=dim), axis, backward)
        block = jnp.concatenate([low, block, high], axis=dim)
    return block


def tap_value(offset, taps):
    total = jnp.zeros(offset.shape, jnp.float32)
    for position in range(8):
        total = total + jnp.where(offset == position, taps[position], 0.0).astype(jnp.float32)
    return total


def fourier_tables(length):
    index = jnp.arange(length, dtype=jnp.int32)
    product = index[:, None] * index[None, :] % length
    angle = product.astype(jnp.float32) * (2.0 * math.pi / length)
    scale = 1.0 / math.sqrt(length)
    return (
        (jnp.cos(angle) * scale).astype(jnp.bfloat16),
        (jnp.sin(angle) * scale).astype(jnp.bfloat16),
    )


def row_matrix(count):
    half = count // 2
    line = jnp.arange(count + 2 * HALO, dtype=jnp.int32)[:, None]
    column = jnp.arange(count, dtype=jnp.int32)[None, :]
    offset = line - 2 * (column % half)
    return jnp.where(column < half, tap_value(offset, low_taps), tap_value(offset, high_taps))


def facet_mask(count, width):
    line = jnp.arange(count + 2 * HALO, dtype=jnp.int32)
    distance = jnp.maximum(jnp.maximum(HALO - line, line - count - HALO + 1), 0)
    return (distance[None, :] <= width[:, None]).astype(jnp.float32)


def column_forward(values):
    width = values.shape[1]
    half = width // 2
    padded = jnp.pad(values, ((0, 0), (HALO, 8)))
    even_cells = padded[:, 0::2]
    odd_cells = padded[:, 1::2]
    low_part = jnp.zeros((values.shape[0], half), jnp.float32)
    high_part = jnp.zeros((values.shape[0], half), jnp.float32)
    for position in range(8):
        source = even_cells if position % 2 == 0 else odd_cells
        piece = source[:, position // 2 : position // 2 + half]
        low_part = low_part + low_taps[position] * piece
        high_part = high_part + high_taps[position] * piece
    return jnp.concatenate([low_part, high_part], axis=1)


def column_adjoint(coefs):
    width = coefs.shape[1]
    half = width // 2
    low_part = coefs[:, :half]
    high_part = coefs[:, half:]
    even_sums = jnp.zeros((coefs.shape[0], half + 4), jnp.float32)
    odd_sums = jnp.zeros((coefs.shape[0], half + 4), jnp.float32)
    for position in range(8):
        term = low_taps[position] * low_part + high_taps[position] * high_part
        placed = jnp.pad(term, ((0, 0), (position // 2, 4 - position // 2)))
        if position % 2 == 0:
            even_sums = even_sums + placed
        else:
            odd_sums = odd_sums + placed
    joined = jnp.stack([even_sums, odd_sums], axis=2).reshape(coefs.shape[0], width + 8)
    return joined[:, HALO : HALO + width]


def data_part(lifted, dual, seen, places, gains, cos_table, sin_table):
    flat_b = lifted.astype(jnp.bfloat16)
    spectra = jnp.stack(
        [
            jnp.dot(flat_b, cos_table, preferred_element_type=jnp.float32),
            -jnp.dot(flat_b, sin_table, preferred_element_type=jnp.float32),
        ]
    ).astype(jnp.bfloat16)
    columns = lax.all_to_all(spectra, "slab", split_axis=2, concat_axis=1, tiled=True)
    grid_real = lax.dot_general(
        columns[0], cos_table, leading, preferred_element_type=jnp.float32
    ) + lax.dot_general(columns[1], sin_table, leading, preferred_element_type=jnp.float32)
    grid_imag = lax.dot_general(
        columns[1], cos_table, leading, preferred_element_type=jnp.float32
    ) - lax.dot_general(columns[0], sin_table, leading, preferred_element_type=jnp.float32)
    model = jnp.stack(
        [gains * grid_real.reshape(-1)[places], gains * grid_imag.reshape(-1)[places]]
    )
    fresh_dual = (dual + (model - seen)) / 2.0
    weighted = gains[None, :] * fresh_dual
    cell_count = grid_real.size
    hold_real = (
        jnp.zeros((cell_count,), jnp.float32)
        .at[places]
        .add(weighted[0])
        .reshape(grid_real.shape)
        .astype(jnp.bfloat16)
    )
    hold_imag = (
        jnp.zeros((cell_count,), jnp.float32)
        .at[places]
        .add(weighted[1])
        .reshape(grid_real.shape)
        .astype(jnp.bfloat16)
    )
    backward = jnp.stack(
        [
            jnp.dot(hold_real, cos_table, preferred_element_type=jnp.float32)
            - jnp.dot(hold_imag, sin_table, preferred_element_type=jnp.float32),
            jnp.dot(hold_real, sin_table, preferred_element_type=jnp.float32)
            + jnp.dot(hold_imag, cos_table, preferred_element_type=jnp.float32),
        ]
    ).astype(jnp.bfloat16)
    returned = lax.all_to_all(backward, "slab", split_axis=2, concat_axis=1, tiled=True)
    data_term = lax.dot_general(
        returned[0], cos_table, leading, preferred_element_type=jnp.float32
    ) - lax.dot_general(returned[1], sin_table, leading, preferred_element_type=jnp.float32)
    return (data_term, fresh_dual)


def wave_part(lifted, row_map, mask):
    highest = lax.Precision.HIGHEST
    count = lifted.shape[0]
    extended = with_halo(lifted, (("slab", 0),), HALO) * mask
    filtered = column_forward(extended)
    coef = lax.dot_general(
        row_map, filtered, leading, precision=highest, preferred_element_type=jnp.float32
    )
    squares = coef * coef
    share = lax.psum_scatter(
        squares.astype(jnp.bfloat16), "chan", scatter_dimension=1, tiled=True
    ).astype(jnp.float32)
    partial_factor = bound_level / jnp.maximum(jnp.sqrt(share), bound_level)
    factor = lax.all_gather(partial_factor, "chan", axis=1, tiled=True)
    fresh_dual = coef * factor
    back = column_adjoint(fresh_dual)
    spread = jnp.dot(row_map, back, precision=highest, preferred_element_type=jnp.float32) * mask
    bands = jnp.concatenate([spread[:HALO], spread[count + HALO :]], axis=0)
    arrived = with_halo(bands, (("slab", 0),), HALO)
    inner = spread[HALO : count + HALO]
    inner = inner.at[:HALO].add(arrived[:HALO])
    inner = inner.at[count - HALO :].add(arrived[3 * HALO :])
    return (inner, fresh_dual)


def local_plain(image, margin, cells, weights, observed, dual_start):
    count = image.shape[1]
    cos_table, sin_table = fourier_tables(N)
    row_map = row_matrix(count)
    mask = facet_mask(count, margin)[0][:, None]
    places = cells[0]
    gains = weights[0]
    seen = observed[:, 0, :]
    dual = dual_start[:, 0, :]
    estimate = image[0]
    data_term, dual = data_part(estimate, dual, seen, places, gains, cos_table, sin_table)
    wave_term, wave_dual = wave_part(estimate, row_map, mask)
    fresh = jnp.maximum(estimate - tau_step * (data_term + wave_term), 0.0)
    return (fresh[None], dual[:, None, :])


LANES = 128
EDGE = 8
CHUNK = 512
highest = lax.Precision.HIGHEST
crossed = (((1,), (1,)), ((), ()))


def pick(offset, taps):
    inside = (offset >= 0) & (offset < 8)
    return np.where(inside, np.asarray(taps, np.float64)[np.clip(offset, 0, 7)], 0.0)


def both_taps(offset, is_low):
    return np.where(is_low, pick(offset, low_taps), pick(offset, high_taps)).astype(np.float32)


def base_tables(length):
    index = np.arange(length)[:, None] * np.arange(LANES)[None, :] % length
    angle = index * (2.0 * np.pi / length)
    scale = 1.0 / np.sqrt(length)
    return np.stack([np.cos(angle) * scale, np.sin(angle) * scale]).astype(np.float32)


def turn_tables(length):
    blocks = length // LANES
    turns = np.arange(blocks)[:, None] * np.arange(blocks)[None, :] % blocks
    angle = turns * (2.0 * np.pi / blocks)
    values = np.stack([np.cos(angle), np.sin(angle)])[..., None]
    return np.broadcast_to(values, (2, blocks, blocks, LANES)).astype(np.float32)


def analysis_map():
    line = np.arange(4 * LANES)[:, None]
    column = np.arange(2 * LANES)[None, :]
    offset = line - (LANES - HALO) - 2 * (column % LANES)
    return both_taps(offset, column < LANES)


def synthesis_map():
    line = np.arange(6 * LANES)[:, None]
    column = np.arange(2 * LANES)[None, :]
    block = line // (2 * LANES) - 1
    offset = column - 2 * LANES * block - 2 * (line % LANES) + HALO
    return both_taps(offset, line % (2 * LANES) < LANES)


def wide_row_map(count):
    half = count // 2
    line = np.arange(count + 2 * EDGE)[:, None] - (EDGE - HALO)
    column = np.arange(count)[None, :]
    offset = line - 2 * (column % half)
    return both_taps(offset, column < half)


def in_two(values):
    top = values.astype(jnp.bfloat16)
    return np.stack([top, (values - top.astype(np.float32)).astype(jnp.bfloat16)])


def split(value):
    top = value.astype(jnp.bfloat16)
    return top, (value - top.astype(jnp.float32)).astype(jnp.bfloat16)


def fine_dot(left, right):
    total = jnp.dot(left[0], right[0], preferred_element_type=jnp.float32)
    total = total + jnp.dot(left[1], right[0], preferred_element_type=jnp.float32)
    return total + jnp.dot(left[0], right[1], preferred_element_type=jnp.float32)


def flip(place, bits):
    result = place
    for bit in (1, 2, 4):
        if bits & bit:
            result = result + bit - 2 * bit * (place // bit % 2)
    return result


def whole_kernel(
    n, c, img_far, margin_far, cells_far, gains_far, seen_far, dual_far, base_far, turn_far, m1_far,
    m2_far, rows_far, rows_t_far,
    out, vout, img, margin, cells, gains, seen, dual, base, turn, m1, m2, rows, rows_t, fetched,
    found_half,
    tc, ts, hot, send1, recv1, send2, recv2, padded, halo, coef, sq, sq_in, cpad, spread, bands,
    grid, marks, hold, u_spot,
    sa, ra, sb, rb, sh, rh, ss, rs, sd, rd,
):
    me = lax.axis_index("slab")
    ch = lax.axis_index("chan")
    count, width = img.shape
    blocks = width // LANES
    vis = cells.shape[1]
    after, before = lax.rem(me + 1, n), lax.rem(me + n - 1, n)

    fetches = [
        pltpu.make_async_copy(far, near, fetched.at[i])
        for i, (far, near) in enumerate(
            [
                (base_far, base), (turn_far, turn), (img_far, img), (cells_far, cells),
                (m1_far, m1), (rows_t_far, rows_t), (margin_far, margin), (rows_far, rows),
                (gains_far, gains), (seen_far, seen), (dual_far, dual), (m2_far, m2),
            ]
        )
    ]
    for fetch in fetches:
        fetch.start()

    barrier = pltpu.get_barrier_semaphore()
    for d in range(1, n):
        pl.semaphore_signal(
            barrier, inc=1, device_id={"slab": lax.rem(me + d, n)},
            device_id_type=pl.DeviceIdType.MESH,
        )
    for d in range(1, c):
        pl.semaphore_signal(
            barrier, inc=1, device_id={"chan": lax.rem(ch + d, c)},
            device_id_type=pl.DeviceIdType.MESH,
        )

    def remote(src, dst, s, r, where):
        return pltpu.make_async_remote_copy(
            src_ref=src, dst_ref=dst, send_sem=s, recv_sem=r, device_id=where,
            device_id_type=pl.DeviceIdType.MESH,
        )

    for fetch in fetches[:2]:
        fetch.wait()
    base_c = base[0].reshape(width // 8, 8, LANES)
    base_s = base[1].reshape(width // 8, 8, LANES)
    for b in range(blocks):
        kc, ks = turn[0, b][None], turn[1, b][None]
        here = slice(b * LANES, (b + 1) * LANES)
        tc[:, here] = (base_c * kc - base_s * ks).reshape(width, LANES).astype(jnp.bfloat16)
        ts[:, here] = (base_s * kc + base_c * ks).reshape(width, LANES).astype(jnp.bfloat16)

    fetches[2].wait()
    flat_b = img[...].astype(jnp.bfloat16)
    part = count // 2
    spec = lax.dot_general(tc[...], flat_b, crossed, preferred_element_type=jnp.float32)
    send1[:, :, :part, :] = spec.astype(jnp.bfloat16).reshape(n, 2, part, count)
    spec = lax.dot_general(ts[...], flat_b, crossed, preferred_element_type=jnp.float32)
    send1[:, :, part:, :] = (-spec).astype(jnp.bfloat16).reshape(n, 2, part, count)

    pl.semaphore_wait(barrier, n + c - 2)
    up = remote(img.at[count - EDGE :], halo.at[0], sh.at[0], rh.at[0], {"slab": after})
    down = remote(img.at[:EDGE], halo.at[1], sh.at[1], rh.at[1], {"slab": before})
    up.start()
    down.start()
    sends1 = []
    for h in range(2):
        for d in range(n - 1, 0, -1):
            peer = flip(me, d)
            copy = remote(
                send1.at[peer, h], recv1.at[me, h], sa.at[h, d], ra.at[h, me], {"slab": peer}
            )
            copy.start()
            sends1.append(copy)
    recv1[me] = send1[me]

    fetches[3].wait()
    spot = cells[...]
    low_spot = spot % width
    step = 32

    def make_hot(i, carry):
        line = lax.broadcasted_iota(jnp.int32, (step, vis), 0) + i * step
        hit = jnp.where(line == low_spot, 1.0, 0.0).astype(jnp.bfloat16)
        hot[pl.ds(pl.multiple_of(i * step, step), step), :] = hit
        return carry

    lax.fori_loop(0, width // step, make_hot, 0)

    tall = count + 2 * EDGE

    def keep(shape, dim):
        line = lax.broadcasted_iota(jnp.int32, shape, dim)
        distance = jnp.maximum(jnp.maximum(EDGE - line, line - count - EDGE + 1), 0)
        return jnp.where(distance <= reach, 1.0, 0.0)

    for fetch in fetches[4:]:
        fetch.wait()
    reach = margin[0]
    row_fwd = split(rows_t[...] * keep((count, tall), 1))
    row_adj = split(rows[...] * keep((tall, count), 0))

    padded[:, :LANES] = jnp.zeros((tall, LANES), jnp.float32)
    padded[:, LANES + width :] = jnp.zeros((tall, LANES), jnp.float32)
    padded[EDGE : EDGE + count, LANES : LANES + width] = img[...]
    up.wait_recv()
    down.wait_recv()
    padded[:EDGE, LANES : LANES + width] = jnp.where(me > 0, halo[0], 0.0)
    padded[EDGE + count :, LANES : LANES + width] = jnp.where(me < n - 1, halo[1], 0.0)
    pair = 2 * LANES
    for b in range(width // pair):
        filtered = fine_dot(split(padded[:, b * pair : b * pair + 4 * LANES]), m1)
        piece = fine_dot(row_fwd, split(filtered))
        coef[:, b * pair : (b + 1) * pair] = piece
        sq[:, b * pair : (b + 1) * pair] = (piece * piece).astype(jnp.bfloat16)
    sends_q = []
    for d in range(1, c):
        peer = lax.rem(ch + d, c)
        copy = remote(sq, sq_in.at[ch], ss.at[d], rs.at[ch], {"chan": peer})
        copy.start()
        sends_q.append(copy)
    sq_in[ch] = sq[...]

    u_spot[...] = spot // width

    def look(h, here):
        found = jnp.dot(grid[h], hot[:, here], preferred_element_type=jnp.float32)
        found = found[:count] + found[count:]
        line = lax.broadcasted_iota(jnp.int32, (part, CHUNK), 0) + h * part
        match = line == u_spot[:, here]
        return [
            jnp.sum(
                jnp.where(match, found[k * part : (k + 1) * part], 0.0), axis=0, keepdims=True
            )
            for k in range(2)
        ]

    def visit_first(i, carry):
        here = pl.ds(pl.multiple_of(i * CHUNK, CHUNK), CHUNK)
        values = look(0, here)
        for k in range(2):
            found_half[k, :, here] = values[k]
        return carry

    def visit_last(i, carry):
        here = pl.ds(pl.multiple_of(i * CHUNK, CHUNK), CHUNK)
        values = look(1, here)
        line = lax.broadcasted_iota(jnp.int32, (count, CHUNK), 0)
        match = line == u_spot[:, here]
        gain = gains[:, here]
        for k in range(2):
            value = values[k] + found_half[k, :, here]
            fresh = (dual[k, :, here] + (gain * value - seen[k, :, here])) / 2.0
            vout[k, :, here] = fresh
            marks[k * count : (k + 1) * count, here] = jnp.where(
                match, gain * fresh, 0.0
            ).astype(jnp.bfloat16)
        return carry

    for h in range(2):
        for d in range(n - 1, 0, -1):
            src = flip(me, d)
            remote(
                send1.at[src, h], recv1.at[src, h], sa.at[h, d], ra.at[h, src], {"slab": src}
            ).wait_recv()
        columns = jnp.concatenate([recv1[j, h] for j in range(n)], axis=1)
        by_cos = jnp.dot(columns, tc[...], preferred_element_type=jnp.float32)
        by_sin = jnp.dot(columns, ts[...], preferred_element_type=jnp.float32)
        values = jnp.concatenate(
            [by_cos[:part] + by_sin[part:], by_cos[part:] - by_sin[:part]], axis=0
        )
        grid[h] = jnp.concatenate(split(values), axis=0)
        lax.fori_loop(0, vis // CHUNK, (visit_first, visit_last)[h], 0, unroll=2)

    def collect(i, carry):
        here = pl.ds(pl.multiple_of(i * pair, pair), pair)
        hold[here, :] = lax.dot_general(
            hot[here, :], marks[...], crossed, preferred_element_type=jnp.float32
        ).astype(jnp.bfloat16)
        return carry

    lax.fori_loop(0, width // pair, collect, 0)

    sends2 = []
    for d in range(n - 1, -1, -1):
        peer = flip(me, d)
        here = pl.ds(pl.multiple_of(peer * count, count), count)
        by_cos = jnp.dot(tc[here, :], hold[...], preferred_element_type=jnp.float32)
        by_sin = jnp.dot(ts[here, :], hold[...], preferred_element_type=jnp.float32)
        real = (by_cos[:, :count] - by_sin[:, count:]).astype(jnp.bfloat16)
        imag = (by_sin[:, :count] + by_cos[:, count:]).astype(jnp.bfloat16)
        if d > 0:
            send2[peer, :, :count] = real
            send2[peer, :, count:] = imag
            copy = remote(send2.at[peer], recv2.at[me], sb.at[d], rb.at[me], {"slab": peer})
            copy.start()
            sends2.append(copy)
        else:
            recv2[me, :, :count] = real
            recv2[me, :, count:] = imag

    for d in range(1, c):
        src = lax.rem(ch + d, c)
        remote(sq, sq_in.at[src], ss.at[d], rs.at[src], {"chan": src}).wait_recv()
    cpad[:, :pair] = jnp.zeros((count, pair), jnp.float32)
    cpad[:, pair + width :] = jnp.zeros((count, pair), jnp.float32)
    for b in range(width // pair):
        here = slice(b * pair, (b + 1) * pair)
        total = sq_in[0, :, here].astype(jnp.float32)
        for j in range(1, c):
            total = total + sq_in[j, :, here].astype(jnp.float32)
        factor = bound_level / jnp.maximum(jnp.sqrt(total), bound_level)
        cpad[:, (b + 1) * pair : (b + 2) * pair] = coef[:, here] * factor
    for b in range(width // pair):
        back = fine_dot(split(cpad[:, b * pair : b * pair + 6 * LANES]), m2)
        spread[:, b * pair : (b + 1) * pair] = fine_dot(row_adj, split(back))
    over = remote(spread.at[count + EDGE :], bands.at[0], sd.at[0], rd.at[0], {"slab": after})
    under = remote(spread.at[:EDGE], bands.at[1], sd.at[1], rd.at[1], {"slab": before})
    over.start()
    under.start()

    side = n // 2
    term = None
    for far in range(2):
        for d in range(1 - far, side):
            src = flip(me, d + far * side)
            remote(
                send2.at[src], recv2.at[src], sb.at[d + far * side], rb.at[src], {"slab": src}
            ).wait_recv()
        first = (me // side + far) % 2 * side
        real = jnp.concatenate([recv2[first + j, :, :count] for j in range(side)], axis=1)
        imag = jnp.concatenate([recv2[first + j, :, count:] for j in range(side)], axis=1)
        here = pl.ds(pl.multiple_of(first * count, count), side * count)
        more = jnp.dot(real, tc[here, :], preferred_element_type=jnp.float32)
        more = more - jnp.dot(imag, ts[here, :], preferred_element_type=jnp.float32)
        term = more if term is None else term + more
    over.wait_recv()
    under.wait_recv()
    wave_first = spread[EDGE : 2 * EDGE, :] + jnp.where(me > 0, bands[0], 0.0)
    wave_last = spread[count : count + EDGE, :] + jnp.where(me < n - 1, bands[1], 0.0)
    wave = jnp.concatenate(
        [wave_first, spread[2 * EDGE : count, :], wave_last], axis=0
    )
    out[...] = jnp.maximum(img[...] - tau_step * (term + wave), 0.0)

    for copy in [up, down, over, under] + sends1 + sends_q + sends2:
        copy.wait_send()


def local_kernel(n, c, image, margin, cells, weights, observed, dual_start):
    count, width = image.shape[1], image.shape[2]
    vis = cells.shape[1]
    tall = count + 2 * EDGE
    half_t, f32 = jnp.bfloat16, jnp.float32
    V = pltpu.VMEM
    dma = pltpu.SemaphoreType.DMA
    row_map = wide_row_map(count)
    vm = pl.BlockSpec(memory_space=pltpu.VMEM)
    fresh, dual = pl.pallas_call(
        functools.partial(whole_kernel, n, c),
        out_shape=(
            jax.ShapeDtypeStruct((count, width), f32),
            jax.ShapeDtypeStruct((2, 1, vis), f32),
        ),
        in_specs=[pl.BlockSpec(memory_space=pl.ANY)] * 12,
        out_specs=(vm, vm),
        scratch_shapes=[
            V((count, width), f32),
            pltpu.SMEM((1,), jnp.int32),
            V((1, vis), jnp.int32),
            V((1, vis), f32),
            V((2, 1, vis), f32),
            V((2, 1, vis), f32),
            V((2, width, LANES), f32),
            V((2, n, n, LANES), f32),
            V((2, 4 * LANES, 2 * LANES), half_t),
            V((2, 6 * LANES, 2 * LANES), half_t),
            V((tall, count), f32),
            V((count, tall), f32),
            dma((12,)),
            V((2, 1, vis), f32),
            V((width, width), half_t),
            V((width, width), half_t),
            V((width, vis), half_t),
            V((n, 2, count, count), half_t),
            V((n, 2, count, count), half_t),
            V((n, count, 2 * count), half_t),
            V((n, count, 2 * count), half_t),
            V((tall, width + 2 * LANES), f32),
            V((2, EDGE, width), f32),
            V((count, width), f32),
            V((count, width), half_t),
            V((c, count, width), half_t),
            V((count, width + 4 * LANES), f32),
            V((tall, width), f32),
            V((2, EDGE, width), f32),
            V((2, 2 * count, width), half_t),
            V((2 * count, vis), half_t),
            V((width, 2 * count), half_t),
            V((1, vis), jnp.int32),
            dma((2, n)), dma((2, n)), dma((n,)), dma((n,)), dma((2,)), dma((2,)),
            dma((c,)), dma((c,)), dma((2,)), dma((2,)),
        ],
        compiler_params=pltpu.CompilerParams(
            collective_id=0, has_side_effects=True, vmem_limit_bytes=60 * 1024 * 1024
        ),
    )(
        image[0], margin, cells, weights, observed, dual_start,
        base_tables(width), turn_tables(width), in_two(analysis_map()), in_two(synthesis_map()),
        row_map, np.ascontiguousarray(row_map.T),
    )
    return (fresh[None], dual)


def solution(mesh):
    n, c = mesh.shape["slab"], mesh.shape["chan"]

    def local(image, *rest):
        count, width = image.shape[1], image.shape[2]
        if n == 8 and count == LANES and width == n * count and rest[1].shape[1] % CHUNK == 0:
            return local_kernel(n, c, image, *rest)
        return local_plain(image, *rest)

    in_specs = (
        P("chan", "slab", None),
        P("slab"),
        P("chan", "slab"),
        P("chan", "slab"),
        P(None, "chan", "slab"),
        P(None, "chan", "slab"),
    )
    out_specs = (P("chan", "slab", None), P(None, "chan", "slab"))
    return jax.shard_map(local, mesh=mesh, in_specs=in_specs, out_specs=out_specs, check_vma=False)
```

```python
import functools
import math

import jax
import jax.numpy as jnp
import numpy as np
from jax import lax
from jax.experimental import pallas as pl
from jax.experimental.pallas import tpu as pltpu
from jax.sharding import PartitionSpec as P

N = 1024
HALO = 3


low_taps = (
    -0.010597401784997278,
    0.032883011666982945,
    0.030841381835986965,
    -0.18703481171888114,
    -0.02798376941698385,
    0.6308807679295904,
    0.7148465705525415,
    0.23037781330885523,
)
high_taps = (
    -0.23037781330885523,
    0.7148465705525415,
    -0.6308807679295904,
    -0.02798376941698385,
    0.18703481171888114,
    0.030841381835986965,
    -0.032883011666982945,
    -0.010597401784997278,
)
tau_step = 0.5
bound_level = 3.0
leading = (((0,), (0,)), ((), ()))


def with_halo(block, sides, width):
    for axis, dim in sides:
        count = lax.axis_size(axis)
        forward = [(i, i + 1) for i in range(count - 1)]
        backward = [(target, source) for source, target in forward]
        low = lax.ppermute(
            lax.slice_in_dim(block, block.shape[dim] - width, None, axis=dim), axis, forward
        )
        high = lax.ppermute(lax.slice_in_dim(block, 0, width, axis=dim), axis, backward)
        block = jnp.concatenate([low, block, high], axis=dim)
    return block


def tap_value(offset, taps):
    total = jnp.zeros(offset.shape, jnp.float32)
    for position in range(8):
        total = total + jnp.where(offset == position, taps[position], 0.0).astype(jnp.float32)
    return total


def fourier_tables(length):
    index = jnp.arange(length, dtype=jnp.int32)
    product = index[:, None] * index[None, :] % length
    angle = product.astype(jnp.float32) * (2.0 * math.pi / length)
    scale = 1.0 / math.sqrt(length)
    return (
        (jnp.cos(angle) * scale).astype(jnp.bfloat16),
        (jnp.sin(angle) * scale).astype(jnp.bfloat16),
    )


def row_matrix(count):
    half = count // 2
    line = jnp.arange(count + 2 * HALO, dtype=jnp.int32)[:, None]
    column = jnp.arange(count, dtype=jnp.int32)[None, :]
    offset = line - 2 * (column % half)
    return jnp.where(column < half, tap_value(offset, low_taps), tap_value(offset, high_taps))


def facet_mask(count, width):
    line = jnp.arange(count + 2 * HALO, dtype=jnp.int32)
    distance = jnp.maximum(jnp.maximum(HALO - line, line - count - HALO + 1), 0)
    return (distance[None, :] <= width[:, None]).astype(jnp.float32)


def column_forward(values):
    width = values.shape[1]
    half = width // 2
    padded = jnp.pad(values, ((0, 0), (HALO, 8)))
    even_cells = padded[:, 0::2]
    odd_cells = padded[:, 1::2]
    low_part = jnp.zeros((values.shape[0], half), jnp.float32)
    high_part = jnp.zeros((values.shape[0], half), jnp.float32)
    for position in range(8):
        source = even_cells if position % 2 == 0 else odd_cells
        piece = source[:, position // 2 : position // 2 + half]
        low_part = low_part + low_taps[position] * piece
        high_part = high_part + high_taps[position] * piece
    return jnp.concatenate([low_part, high_part], axis=1)


def column_adjoint(coefs):
    width = coefs.shape[1]
    half = width // 2
    low_part = coefs[:, :half]
    high_part = coefs[:, half:]
    even_sums = jnp.zeros((coefs.shape[0], half + 4), jnp.float32)
    odd_sums = jnp.zeros((coefs.shape[0], half + 4), jnp.float32)
    for position in range(8):
        term = low_taps[position] * low_part + high_taps[position] * high_part
        placed = jnp.pad(term, ((0, 0), (position // 2, 4 - position // 2)))
        if position % 2 == 0:
            even_sums = even_sums + placed
        else:
            odd_sums = odd_sums + placed
    joined = jnp.stack([even_sums, odd_sums], axis=2).reshape(coefs.shape[0], width + 8)
    return joined[:, HALO : HALO + width]


def data_part(lifted, dual, seen, places, gains, cos_table, sin_table):
    flat_b = lifted.astype(jnp.bfloat16)
    spectra = jnp.stack(
        [
            jnp.dot(flat_b, cos_table, preferred_element_type=jnp.float32),
            -jnp.dot(flat_b, sin_table, preferred_element_type=jnp.float32),
        ]
    ).astype(jnp.bfloat16)
    columns = lax.all_to_all(spectra, "slab", split_axis=2, concat_axis=1, tiled=True)
    grid_real = lax.dot_general(
        columns[0], cos_table, leading, preferred_element_type=jnp.float32
    ) + lax.dot_general(columns[1], sin_table, leading, preferred_element_type=jnp.float32)
    grid_imag = lax.dot_general(
        columns[1], cos_table, leading, preferred_element_type=jnp.float32
    ) - lax.dot_general(columns[0], sin_table, leading, preferred_element_type=jnp.float32)
    model = jnp.stack(
        [gains * grid_real.reshape(-1)[places], gains * grid_imag.reshape(-1)[places]]
    )
    fresh_dual = (dual + (model - seen)) / 2.0
    weighted = gains[None, :] * fresh_dual
    cell_count = grid_real.size
    hold_real = (
        jnp.zeros((cell_count,), jnp.float32)
        .at[places]
        .add(weighted[0])
        .reshape(grid_real.shape)
        .astype(jnp.bfloat16)
    )
    hold_imag = (
        jnp.zeros((cell_count,), jnp.float32)
        .at[places]
        .add(weighted[1])
        .reshape(grid_real.shape)
        .astype(jnp.bfloat16)
    )
    backward = jnp.stack(
        [
            jnp.dot(hold_real, cos_table, preferred_element_type=jnp.float32)
            - jnp.dot(hold_imag, sin_table, preferred_element_type=jnp.float32),
            jnp.dot(hold_real, sin_table, preferred_element_type=jnp.float32)
            + jnp.dot(hold_imag, cos_table, preferred_element_type=jnp.float32),
        ]
    ).astype(jnp.bfloat16)
    returned = lax.all_to_all(backward, "slab", split_axis=2, concat_axis=1, tiled=True)
    data_term = lax.dot_general(
        returned[0], cos_table, leading, preferred_element_type=jnp.float32
    ) - lax.dot_general(returned[1], sin_table, leading, preferred_element_type=jnp.float32)
    return (data_term, fresh_dual)


def wave_part(lifted, row_map, mask):
    highest = lax.Precision.HIGHEST
    count = lifted.shape[0]
    extended = with_halo(lifted, (("slab", 0),), HALO) * mask
    filtered = column_forward(extended)
    coef = lax.dot_general(
        row_map, filtered, leading, precision=highest, preferred_element_type=jnp.float32
    )
    squares = coef * coef
    share = lax.psum_scatter(
        squares.astype(jnp.bfloat16), "chan", scatter_dimension=1, tiled=True
    ).astype(jnp.float32)
    partial_factor = bound_level / jnp.maximum(jnp.sqrt(share), bound_level)
    factor = lax.all_gather(partial_factor, "chan", axis=1, tiled=True)
    fresh_dual = coef * factor
    back = column_adjoint(fresh_dual)
    spread = jnp.dot(row_map, back, precision=highest, preferred_element_type=jnp.float32) * mask
    bands = jnp.concatenate([spread[:HALO], spread[count + HALO :]], axis=0)
    arrived = with_halo(bands, (("slab", 0),), HALO)
    inner = spread[HALO : count + HALO]
    inner = inner.at[:HALO].add(arrived[:HALO])
    inner = inner.at[count - HALO :].add(arrived[3 * HALO :])
    return (inner, fresh_dual)


def local_plain(image, margin, cells, weights, observed, dual_start):
    count = image.shape[1]
    cos_table, sin_table = fourier_tables(N)
    row_map = row_matrix(count)
    mask = facet_mask(count, margin)[0][:, None]
    places = cells[0]
    gains = weights[0]
    seen = observed[:, 0, :]
    dual = dual_start[:, 0, :]
    estimate = image[0]
    data_term, dual = data_part(estimate, dual, seen, places, gains, cos_table, sin_table)
    wave_term, wave_dual = wave_part(estimate, row_map, mask)
    fresh = jnp.maximum(estimate - tau_step * (data_term + wave_term), 0.0)
    return (fresh[None], dual[:, None, :])


LANES = 128
EDGE = 8
CHUNK = 512
highest = lax.Precision.HIGHEST
crossed = (((1,), (1,)), ((), ()))


def pick(offset, taps):
    inside = (offset >= 0) & (offset < 8)
    return np.where(inside, np.asarray(taps, np.float64)[np.clip(offset, 0, 7)], 0.0)


def both_taps(offset, is_low):
    return np.where(is_low, pick(offset, low_taps), pick(offset, high_taps)).astype(np.float32)


def base_tables(length):
    index = np.arange(length)[:, None] * np.arange(LANES)[None, :] % length
    angle = index * (2.0 * np.pi / length)
    scale = 1.0 / np.sqrt(length)
    return np.stack([np.cos(angle) * scale, np.sin(angle) * scale]).astype(np.float32)


def turn_tables(length):
    blocks = length // LANES
    turns = np.arange(blocks)[:, None] * np.arange(blocks)[None, :] % blocks
    angle = turns * (2.0 * np.pi / blocks)
    values = np.stack([np.cos(angle), np.sin(angle)])[..., None]
    return np.broadcast_to(values, (2, blocks, blocks, LANES)).astype(np.float32)


def analysis_map():
    line = np.arange(4 * LANES)[:, None]
    column = np.arange(2 * LANES)[None, :]
    offset = line - (LANES - HALO) - 2 * (column % LANES)
    return both_taps(offset, column < LANES)


def synthesis_map():
    line = np.arange(6 * LANES)[:, None]
    column = np.arange(2 * LANES)[None, :]
    block = line // (2 * LANES) - 1
    offset = column - 2 * LANES * block - 2 * (line % LANES) + HALO
    return both_taps(offset, line % (2 * LANES) < LANES)


def wide_row_map(count):
    half = count // 2
    line = np.arange(count + 2 * EDGE)[:, None] - (EDGE - HALO)
    column = np.arange(count)[None, :]
    offset = line - 2 * (column % half)
    return both_taps(offset, column < half)


def in_two(values):
    top = values.astype(jnp.bfloat16)
    return np.stack([top, (values - top.astype(np.float32)).astype(jnp.bfloat16)])


def split(value):
    top = value.astype(jnp.bfloat16)
    return top, (value - top.astype(jnp.float32)).astype(jnp.bfloat16)


def fine_dot(left, right):
    total = jnp.dot(left[0], right[0], preferred_element_type=jnp.float32)
    total = total + jnp.dot(left[1], right[0], preferred_element_type=jnp.float32)
    return total + jnp.dot(left[0], right[1], preferred_element_type=jnp.float32)


def flip(place, bits):
    result = place
    for bit in (1, 2, 4):
        if bits & bit:
            result = result + bit - 2 * bit * (place // bit % 2)
    return result


def whole_kernel(
    n, c, img, margin, cells, gains, seen, dual, base, turn, m1_far, m2_far, rows_far, rows_t_far,
    out, vout, m1, m2, rows, rows_t, fetched, found_half,
    tc, ts, hot, send1, recv1, send2, recv2, padded, halo, coef, sq, sq_in, cpad, spread, bands,
    grid, marks, hold, u_spot,
    sa, ra, sb, rb, sh, rh, ss, rs, sd, rd,
):
    me = lax.axis_index("slab")
    ch = lax.axis_index("chan")
    count, width = img.shape
    blocks = width // LANES
    vis = cells.shape[1]
    after, before = lax.rem(me + 1, n), lax.rem(me + n - 1, n)

    barrier = pltpu.get_barrier_semaphore()
    for d in range(1, n):
        pl.semaphore_signal(
            barrier, inc=1, device_id={"slab": lax.rem(me + d, n)},
            device_id_type=pl.DeviceIdType.MESH,
        )
    for d in range(1, c):
        pl.semaphore_signal(
            barrier, inc=1, device_id={"chan": lax.rem(ch + d, c)},
            device_id_type=pl.DeviceIdType.MESH,
        )

    def remote(src, dst, s, r, where):
        return pltpu.make_async_remote_copy(
            src_ref=src, dst_ref=dst, send_sem=s, recv_sem=r, device_id=where,
            device_id_type=pl.DeviceIdType.MESH,
        )

    fetches = [
        pltpu.make_async_copy(far, near, fetched.at[i])
        for i, (far, near) in enumerate(
            [(m1_far, m1), (rows_far, rows), (rows_t_far, rows_t), (m2_far, m2)]
        )
    ]
    for fetch in fetches:
        fetch.start()

    base_c = base[0].reshape(width // 8, 8, LANES)
    base_s = base[1].reshape(width // 8, 8, LANES)
    for b in range(blocks):
        kc, ks = turn[0, b][None], turn[1, b][None]
        here = slice(b * LANES, (b + 1) * LANES)
        tc[:, here] = (base_c * kc - base_s * ks).reshape(width, LANES).astype(jnp.bfloat16)
        ts[:, here] = (base_s * kc + base_c * ks).reshape(width, LANES).astype(jnp.bfloat16)

    flat_b = img[...].astype(jnp.bfloat16)
    part = count // 2
    spec = lax.dot_general(tc[...], flat_b, crossed, preferred_element_type=jnp.float32)
    send1[:, :, :part, :] = spec.astype(jnp.bfloat16).reshape(n, 2, part, count)
    spec = lax.dot_general(ts[...], flat_b, crossed, preferred_element_type=jnp.float32)
    send1[:, :, part:, :] = (-spec).astype(jnp.bfloat16).reshape(n, 2, part, count)

    pl.semaphore_wait(barrier, n + c - 2)
    up = remote(img.at[count - EDGE :], halo.at[0], sh.at[0], rh.at[0], {"slab": after})
    down = remote(img.at[:EDGE], halo.at[1], sh.at[1], rh.at[1], {"slab": before})
    up.start()
    down.start()
    sends1 = []
    for h in range(2):
        for d in range(n - 1, 0, -1):
            peer = flip(me, d)
            copy = remote(
                send1.at[peer, h], recv1.at[me, h], sa.at[h, d], ra.at[h, me], {"slab": peer}
            )
            copy.start()
            sends1.append(copy)
    recv1[me] = send1[me]

    spot = cells[...]
    low_spot = spot % width
    step = 32

    def make_hot(i, carry):
        line = lax.broadcasted_iota(jnp.int32, (step, vis), 0) + i * step
        hit = jnp.where(line == low_spot, 1.0, 0.0).astype(jnp.bfloat16)
        hot[pl.ds(pl.multiple_of(i * step, step), step), :] = hit
        return carry

    lax.fori_loop(0, width // step, make_hot, 0)

    reach = margin[0]
    tall = count + 2 * EDGE

    def keep(shape, dim):
        line = lax.broadcasted_iota(jnp.int32, shape, dim)
        distance = jnp.maximum(jnp.maximum(EDGE - line, line - count - EDGE + 1), 0)
        return jnp.where(distance <= reach, 1.0, 0.0)

    for fetch in fetches:
        fetch.wait()
    row_fwd = split(rows_t[...] * keep((count, tall), 1))
    row_adj = split(rows[...] * keep((tall, count), 0))

    padded[:, :LANES] = jnp.zeros((tall, LANES), jnp.float32)
    padded[:, LANES + width :] = jnp.zeros((tall, LANES), jnp.float32)
    padded[EDGE : EDGE + count, LANES : LANES + width] = img[...]
    up.wait_recv()
    down.wait_recv()
    padded[:EDGE, LANES : LANES + width] = jnp.where(me > 0, halo[0], 0.0)
    padded[EDGE + count :, LANES : LANES + width] = jnp.where(me < n - 1, halo[1], 0.0)
    pair = 2 * LANES
    for b in range(width // pair):
        filtered = fine_dot(split(padded[:, b * pair : b * pair + 4 * LANES]), m1)
        piece = fine_dot(row_fwd, split(filtered))
        coef[:, b * pair : (b + 1) * pair] = piece
        sq[:, b * pair : (b + 1) * pair] = (piece * piece).astype(jnp.bfloat16)
    sends_q = []
    for d in range(1, c):
        peer = lax.rem(ch + d, c)
        copy = remote(sq, sq_in.at[ch], ss.at[d], rs.at[ch], {"chan": peer})
        copy.start()
        sends_q.append(copy)
    sq_in[ch] = sq[...]

    u_spot[...] = spot // width

    def look(h, here):
        found = jnp.dot(grid[h], hot[:, here], preferred_element_type=jnp.float32)
        found = found[:count] + found[count:]
        line = lax.broadcasted_iota(jnp.int32, (part, CHUNK), 0) + h * part
        match = line == u_spot[:, here]
        return [
            jnp.sum(
                jnp.where(match, found[k * part : (k + 1) * part], 0.0), axis=0, keepdims=True
            )
            for k in range(2)
        ]

    def visit_first(i, carry):
        here = pl.ds(pl.multiple_of(i * CHUNK, CHUNK), CHUNK)
        values = look(0, here)
        for k in range(2):
            found_half[k, :, here] = values[k]
        return carry

    def visit_last(i, carry):
        here = pl.ds(pl.multiple_of(i * CHUNK, CHUNK), CHUNK)
        values = look(1, here)
        line = lax.broadcasted_iota(jnp.int32, (count, CHUNK), 0)
        match = line == u_spot[:, here]
        gain = gains[:, here]
        for k in range(2):
            value = values[k] + found_half[k, :, here]
            fresh = (dual[k, :, here] + (gain * value - seen[k, :, here])) / 2.0
            vout[k, :, here] = fresh
            marks[k * count : (k + 1) * count, here] = jnp.where(
                match, gain * fresh, 0.0
            ).astype(jnp.bfloat16)
        return carry

    for h in range(2):
        for d in range(n - 1, 0, -1):
            src = flip(me, d)
            remote(
                send1.at[src, h], recv1.at[src, h], sa.at[h, d], ra.at[h, src], {"slab": src}
            ).wait_recv()
        columns = jnp.concatenate([recv1[j, h] for j in range(n)], axis=1)
        by_cos = jnp.dot(columns, tc[...], preferred_element_type=jnp.float32)
        by_sin = jnp.dot(columns, ts[...], preferred_element_type=jnp.float32)
        values = jnp.concatenate(
            [by_cos[:part] + by_sin[part:], by_cos[part:] - by_sin[:part]], axis=0
        )
        grid[h] = jnp.concatenate(split(values), axis=0)
        lax.fori_loop(0, vis // CHUNK, (visit_first, visit_last)[h], 0, unroll=2)

    def collect(i, carry):
        here = pl.ds(pl.multiple_of(i * pair, pair), pair)
        hold[here, :] = lax.dot_general(
            hot[here, :], marks[...], crossed, preferred_element_type=jnp.float32
        ).astype(jnp.bfloat16)
        return carry

    lax.fori_loop(0, width // pair, collect, 0)

    sends2 = []
    for d in range(n - 1, -1, -1):
        peer = flip(me, d)
        here = pl.ds(pl.multiple_of(peer * count, count), count)
        by_cos = jnp.dot(tc[here, :], hold[...], preferred_element_type=jnp.float32)
        by_sin = jnp.dot(ts[here, :], hold[...], preferred_element_type=jnp.float32)
        real = (by_cos[:, :count] - by_sin[:, count:]).astype(jnp.bfloat16)
        imag = (by_sin[:, :count] + by_cos[:, count:]).astype(jnp.bfloat16)
        if d > 0:
            send2[peer, :, :count] = real
            send2[peer, :, count:] = imag
            copy = remote(send2.at[peer], recv2.at[me], sb.at[d], rb.at[me], {"slab": peer})
            copy.start()
            sends2.append(copy)
        else:
            recv2[me, :, :count] = real
            recv2[me, :, count:] = imag

    for d in range(1, c):
        src = lax.rem(ch + d, c)
        remote(sq, sq_in.at[src], ss.at[d], rs.at[src], {"chan": src}).wait_recv()
    cpad[:, :pair] = jnp.zeros((count, pair), jnp.float32)
    cpad[:, pair + width :] = jnp.zeros((count, pair), jnp.float32)
    for b in range(width // pair):
        here = slice(b * pair, (b + 1) * pair)
        total = sq_in[0, :, here].astype(jnp.float32)
        for j in range(1, c):
            total = total + sq_in[j, :, here].astype(jnp.float32)
        factor = bound_level / jnp.maximum(jnp.sqrt(total), bound_level)
        cpad[:, (b + 1) * pair : (b + 2) * pair] = coef[:, here] * factor
    for b in range(width // pair):
        back = fine_dot(split(cpad[:, b * pair : b * pair + 6 * LANES]), m2)
        spread[:, b * pair : (b + 1) * pair] = fine_dot(row_adj, split(back))
    over = remote(spread.at[count + EDGE :], bands.at[0], sd.at[0], rd.at[0], {"slab": after})
    under = remote(spread.at[:EDGE], bands.at[1], sd.at[1], rd.at[1], {"slab": before})
    over.start()
    under.start()

    side = n // 2
    term = None
    for far in range(2):
        for d in range(1 - far, side):
            src = flip(me, d + far * side)
            remote(
                send2.at[src], recv2.at[src], sb.at[d + far * side], rb.at[src], {"slab": src}
            ).wait_recv()
        first = (me // side + far) % 2 * side
        real = jnp.concatenate([recv2[first + j, :, :count] for j in range(side)], axis=1)
        imag = jnp.concatenate([recv2[first + j, :, count:] for j in range(side)], axis=1)
        here = pl.ds(pl.multiple_of(first * count, count), side * count)
        more = jnp.dot(real, tc[here, :], preferred_element_type=jnp.float32)
        more = more - jnp.dot(imag, ts[here, :], preferred_element_type=jnp.float32)
        term = more if term is None else term + more
    over.wait_recv()
    under.wait_recv()
    wave_first = spread[EDGE : 2 * EDGE, :] + jnp.where(me > 0, bands[0], 0.0)
    wave_last = spread[count : count + EDGE, :] + jnp.where(me < n - 1, bands[1], 0.0)
    wave = jnp.concatenate(
        [wave_first, spread[2 * EDGE : count, :], wave_last], axis=0
    )
    out[...] = jnp.maximum(img[...] - tau_step * (term + wave), 0.0)

    for copy in [up, down, over, under] + sends1 + sends_q + sends2:
        copy.wait_send()


def local_kernel(n, c, image, margin, cells, weights, observed, dual_start):
    count, width = image.shape[1], image.shape[2]
    vis = cells.shape[1]
    tall = count + 2 * EDGE
    half_t, f32 = jnp.bfloat16, jnp.float32
    V = pltpu.VMEM
    dma = pltpu.SemaphoreType.DMA
    row_map = wide_row_map(count)
    vm = pl.BlockSpec(memory_space=pltpu.VMEM)
    fresh, dual = pl.pallas_call(
        functools.partial(whole_kernel, n, c),
        out_shape=(
            jax.ShapeDtypeStruct((count, width), f32),
            jax.ShapeDtypeStruct((2, 1, vis), f32),
        ),
        in_specs=[vm, pl.BlockSpec(memory_space=pltpu.SMEM)] + [vm] * 6
        + [pl.BlockSpec(memory_space=pl.ANY)] * 4,
        out_specs=(vm, vm),
        scratch_shapes=[
            V((2, 4 * LANES, 2 * LANES), half_t),
            V((2, 6 * LANES, 2 * LANES), half_t),
            V((tall, count), f32),
            V((count, tall), f32),
            dma((4,)),
            V((2, 1, vis), f32),
            V((width, width), half_t),
            V((width, width), half_t),
            V((width, vis), half_t),
            V((n, 2, count, count), half_t),
            V((n, 2, count, count), half_t),
            V((n, count, 2 * count), half_t),
            V((n, count, 2 * count), half_t),
            V((tall, width + 2 * LANES), f32),
            V((2, EDGE, width), f32),
            V((count, width), f32),
            V((count, width), half_t),
            V((c, count, width), half_t),
            V((count, width + 4 * LANES), f32),
            V((tall, width), f32),
            V((2, EDGE, width), f32),
            V((2, 2 * count, width), half_t),
            V((2 * count, vis), half_t),
            V((width, 2 * count), half_t),
            V((1, vis), jnp.int32),
            dma((2, n)), dma((2, n)), dma((n,)), dma((n,)), dma((2,)), dma((2,)),
            dma((c,)), dma((c,)), dma((2,)), dma((2,)),
        ],
        compiler_params=pltpu.CompilerParams(
            collective_id=0, has_side_effects=True, vmem_limit_bytes=60 * 1024 * 1024
        ),
    )(
        image[0], margin, cells, weights, observed, dual_start,
        base_tables(width), turn_tables(width), in_two(analysis_map()), in_two(synthesis_map()),
        row_map, np.ascontiguousarray(row_map.T),
    )
    return (fresh[None], dual)


def solution(mesh):
    n, c = mesh.shape["slab"], mesh.shape["chan"]

    def local(image, *rest):
        count, width = image.shape[1], image.shape[2]
        if n == 8 and count == LANES and width == n * count and rest[1].shape[1] % CHUNK == 0:
            return local_kernel(n, c, image, *rest)
        return local_plain(image, *rest)

    in_specs = (
        P("chan", "slab", None),
        P("slab"),
        P("chan", "slab"),
        P("chan", "slab"),
        P(None, "chan", "slab"),
        P(None, "chan", "slab"),
    )
    out_specs = (P("chan", "slab", None), P(None, "chan", "slab"))
    return jax.shard_map(local, mesh=mesh, in_specs=in_specs, out_specs=out_specs, check_vma=False)
```
